32 devices in a mesh: elec: 4 (over y, core), pix: 8 (over z, x).
Axes of the slice: x: 2, y: 2, z: 4, core: 2. Of those that a mesh axis runs over, the one named last changes fastest.
Arguments:
- wavefronts: bfloat16 [1536, 2, 320, 256], P('elec', None, 'pix'), may hold values from -40 to 40, as said below
- trial_modes: float32 [2, 32, 320, 256], P(None, None, 'pix'), may hold values from -6 to 6
Outputs:
- sample_modes: float32 [2, 32, 320, 256], P(None, 'elec', None, 'pix')
The draws below stay inside these ranges and needn't reach their ends.
Inputs may be any that keep to these rules, and one draw needn't show every extreme that they name: `wavefronts`: field samples of each electron's wavefront.
All inputs are finite; a program needn't handle non-finite values.
Results may differ from the reference program's by a relative error of at most 0.0075.
Values may be sent and summed in bfloat16 or wider, within the bound.
A program may use at most 128 MiB of HBM per device.

```python
import math
import jax
import jax.numpy as jnp
from jax import lax

R = 320
C = 256
MODES = 32
ELEC_DEV = 384
ITERS = 2
NS_STEPS = 8
ELECTRONS = 1536
N_ELEC = 4


def draw_wavefronts(key, part):
    key_samples, key_rows, key_pixels = jax.random.split(key, 3)
    samples = jnp.clip(jax.random.normal(key_samples, (ELECTRONS, 2, R, C), jnp.float32), -4.0, 4.0)
    spread = math.log(10.0) / 2.0
    row_scale = jnp.exp(jax.random.uniform(key_rows, (ELECTRONS, 1, 1, 1), jnp.float32, 0.0, spread))
    pixel_scale = jnp.exp(jax.random.uniform(key_pixels, (1, 1, R, C), jnp.float32, 0.0, spread))
    return (samples * row_scale * pixel_scale).astype(jnp.bfloat16)


def shard_levels(rng, extent, cuts, low, top_value):
    loudness = 1.0
    for dim, shards_of in cuts:
        heights = jax.random.uniform(jax.random.fold_in(jax.random.fold_in(rng, 6), dim), (shards_of,), jnp.float32, low / len(cuts), top_value / len(cuts))
        loudness = loudness * jnp.repeat(jnp.exp(heights), extent[dim] // shards_of).reshape((-1,) + (1,) * (len(extent) - 1 - dim))
    return loudness


def scatter_about(key, extent, scale, bound, cuts=(), kind=jnp.bfloat16):
    loudness = shard_levels(key, extent, cuts, -0.22, 0.18) if cuts else 1.0
    array = jax.random.normal(key, extent, jnp.float32) * scale * loudness
    return jnp.minimum(jnp.maximum(array, -bound), bound).astype(kind)


def setup_inputs(seed: int = 0) -> dict:
    arg_keys = jax.random.split(jax.random.key(seed), 3)
    wavefronts = draw_wavefronts(jax.random.fold_in(arg_keys[2], 71), 0)
    trial_modes = scatter_about(arg_keys[1], (2, MODES, R, C), 1.0, 6.0, ((2, 8),), jnp.float32)
    return {"wavefronts": wavefronts, "trial_modes": trial_modes}


HIGH = lax.Precision.HIGHEST

def project(wave_re, wave_im, modes_low):
    stacked = modes_low.reshape(-1, modes_low.shape[2])
    swapped = jnp.concatenate([-modes_low[1], modes_low[0]], axis=0)
    contract = (((1,), (1,)), ((), ()))
    real_side = lax.dot_general(wave_re, stacked, contract, preferred_element_type=jnp.float32)
    imag_side = lax.dot_general(wave_im, swapped, contract, preferred_element_type=jnp.float32)
    return real_side + imag_side

def covariance(waves, projected, mode_count):
    pixels = waves.shape[1] // 2
    blocks = lax.dot_general(projected, waves.astype(jnp.float32), (((0,), (0,)), ((), ())), precision=HIGH, preferred_element_type=jnp.float32)
    real_part = blocks[:mode_count, :pixels] + blocks[mode_count:, pixels:]
    imag_part = blocks[mode_count:, :pixels] - blocks[:mode_count, pixels:]
    return jnp.stack([real_part, imag_part])

def gram_matrix(fields):
    flat = fields.reshape(-1, fields.shape[2])
    return jnp.dot(flat, flat.T, precision=HIGH)

def lowdin(gram_raw, mode_count):
    gram_re = gram_raw[:mode_count, :mode_count] + gram_raw[mode_count:, mode_count:]
    gram_im = gram_raw[:mode_count, mode_count:] - gram_raw[mode_count:, :mode_count]
    embedded = jnp.concatenate([jnp.concatenate([gram_re, -gram_im], 1), jnp.concatenate([gram_im, gram_re], 1)], 0)
    trace_value = jnp.trace(embedded)
    scaled = embedded / trace_value
    identity = jnp.eye(2 * mode_count, dtype=embedded.dtype)
    inverse_root = identity
    for iteration in range(NS_STEPS):
        correction = 1.5 * identity - 0.5 * jnp.dot(inverse_root, scaled, precision=HIGH)
        scaled = jnp.dot(scaled, correction, precision=HIGH)
        inverse_root = jnp.dot(correction, inverse_root, precision=HIGH)
    return (inverse_root / jnp.sqrt(trace_value)).T

def rotate(rotation, fields):
    flat = fields.reshape(-1, fields.shape[2])
    return jnp.dot(rotation, flat, precision=HIGH).reshape(fields.shape)

def dft_table(length):
    index = jnp.arange(length, dtype=jnp.int32)
    product = index[:, None] * index[None, :] % length
    angle = 2.0 * math.pi / length * product.astype(jnp.float32)
    return (jnp.cos(angle), -jnp.sin(angle))

def chirp_phase(row_pos, col_pos, row_total, col_total, factor):
    row_term = (row_pos - row_total / 2.0) ** 2 / row_total
    col_term = (col_pos - col_total / 2.0) ** 2 / col_total
    angle = math.pi * factor * (row_term[:, None] + col_term[None, :])
    return (jnp.cos(angle), jnp.sin(angle))

def column_section(field, row_pos, row_total, col_total):
    col_pos = jnp.arange(col_total, dtype=jnp.float32)
    chirp_re, chirp_im = chirp_phase(row_pos, col_pos, row_total, col_total, 0.5)
    launch_re = chirp_re * field[0] - chirp_im * field[1]
    launch_im = chirp_re * field[1] + chirp_im * field[0]
    table_re, table_im = dft_table(col_total)
    spec_re = jnp.einsum('mry,yv->mrv', launch_re, table_re, precision=HIGH) - jnp.einsum('mry,yv->mrv', launch_im, table_im, precision=HIGH)
    spec_im = jnp.einsum('mry,yv->mrv', launch_re, table_im, precision=HIGH) + jnp.einsum('mry,yv->mrv', launch_im, table_re, precision=HIGH)
    return jnp.stack([spec_re, spec_im])

def row_section(spectrum, col_pos, row_total, col_total):
    table_re, table_im = dft_table(row_total)
    out_re = jnp.einsum('ux,mxv->muv', table_re, spectrum[0], precision=HIGH) - jnp.einsum('ux,mxv->muv', table_im, spectrum[1], precision=HIGH)
    out_im = jnp.einsum('ux,mxv->muv', table_re, spectrum[1], precision=HIGH) + jnp.einsum('ux,mxv->muv', table_im, spectrum[0], precision=HIGH)
    row_pos = jnp.arange(row_total, dtype=jnp.float32)
    chirp_re, chirp_im = chirp_phase(row_pos, col_pos, row_total, col_total, 0.25)
    return jnp.stack([chirp_re * out_re - chirp_im * out_im, chirp_re * out_im + chirp_im * out_re])

def reference(wavefronts, trial_modes):
    pixels = R * C
    grouped = wavefronts.reshape(N_ELEC, ELEC_DEV, 2 * pixels)
    modes = trial_modes.reshape(2, MODES, pixels)
    for iteration in range(ITERS):
        modes_low = modes.astype(jnp.bfloat16)

        def group_sum(total, waves):
            projected = project(waves[:, :pixels], waves[:, pixels:], modes_low)
            return (total + covariance(waves, projected, MODES), None)
        applied, _ = lax.scan(group_sum, jnp.zeros((2, MODES, pixels), jnp.float32), grouped)
        modes = rotate(lowdin(gram_matrix(applied), MODES), applied)
    field = modes.reshape(2, MODES, R, C)
    spectrum = column_section(field, jnp.arange(R, dtype=jnp.float32), R, C)
    return row_section(spectrum, jnp.arange(C, dtype=jnp.float32), R, C)
```

```python
import functools
import math

import jax
import jax.numpy as jnp
import numpy as np
from jax import lax
from jax.experimental import pallas as pl
from jax.experimental.pallas import tpu as pltpu
from jax.sharding import PartitionSpec as P

NS_STEPS = 8

HIGH = lax.Precision.HIGHEST
MESH = pl.DeviceIdType.MESH
EBLOCK = 128


def greet(*groups):
    barrier = pltpu.get_barrier_semaphore()
    for axis, peers in groups:
        for peer in peers:
            pl.semaphore_signal(barrier, inc=1, device_id={axis: peer}, device_id_type=MESH)
    return sum(len(peers) for _, peers in groups)


def remote(src, dst, send_sem, recv_sem, axis, peer):
    return pltpu.make_async_remote_copy(
        src_ref=src,
        dst_ref=dst,
        send_sem=send_sem,
        recv_sem=recv_sem,
        device_id={axis: peer},
        device_id_type=MESH,
    )


NT = (((1,), (1,)), ((), ()))
NN = (((1,), (0,)), ((), ()))


def dot(left, right, dims):
    return lax.dot_general(left, right, dims, preferred_element_type=jnp.float32)


def scatter_gather(n, peers, x_ref, held, out_ref, send_a, recv_a, send_b, recv_b):
    me = lax.axis_index("pix")
    started = []
    scatter = []
    for d in range(1, n):
        peer = peers[d - 1]
        copy = remote(x_ref.at[peer], held.at[d], send_a.at[d], recv_a.at[d], "pix", peer)
        copy.start()
        scatter.append(copy)
    total = x_ref[me]
    for d in range(1, n):
        scatter[d - 1].wait_recv()
        total = total + held[d]
    out_ref[me] = total
    for d in range(1, n):
        copy = remote(
            out_ref.at[me], out_ref.at[me], send_b.at[d], recv_b.at[d], "pix", peers[d - 1]
        )
        copy.start()
        started.append(copy)
    for d in range(1, n):
        source = lax.rem(me + n - d, n)
        block = out_ref.at[source]
        remote(block, block, send_b.at[d], recv_b.at[d], "pix", source).wait_recv()
    return scatter + started


def core_kernel(
    np_, ne, pieces, sub, electrons, modes, raw,
    waves_hbm, trial_hbm, chirp_hbm, table_hbm,
    out_ref,
    stage_ref, waves_ref, trial_ref, low_ref, chirp_ref, table_ref, pick_ref,
    applied_ref, turn_ref, part_ref, lines_ref, launch_ref, spec_ref, send_ref, rows_a, both_ref, cut_ref, emb_ref,
    held_a, total_a, pay_ref, held_b, total_b,
    x_ref, pair, half, far, first_ref, gram_in,
    ps, es, gs, load_sem,
):
    share = modes // ne
    rows, cols = chirp_ref.shape[1:]
    pixels = rows * cols
    lines = sub // cols
    order = 2 * modes
    chunk = order // ne
    depth = order // np_
    width = pixels // pieces
    me_p = lax.axis_index("pix")
    peers = [lax.rem(me_p + d, np_) for d in range(1, np_)]
    me = lax.axis_index("elec")
    core = lax.rem(me, 2)
    chip = me // 2
    chips = ne // 2
    partner = chip * 2 + 1 - core
    others = [lax.rem(chip + d, chips) for d in range(1, chips)]
    seats = [other * 2 + core for other in others]
    sources = [lax.rem(chip + chips - d, chips) for d in range(1, chips)]
    greeted = greet(("pix", peers), ("elec", [partner] + seats))
    rows_a[...] = jnp.zeros_like(rows_a)

    def load(src, dst, slot):
        copy = pltpu.make_async_copy(src, dst, load_sem.at[slot])
        copy.start()
        return copy

    panels = cols // 128
    trial_copies = [
        load(trial_hbm.at[:, pl.ds(b * 128, 128)], trial_ref.at[b], 2 + b) for b in range(panels)
    ]
    if raw:
        band, batch = 8, EBLOCK
        blocks = electrons // batch

        def wave_copy(step):
            block, half_of = step // 2, lax.rem(step, 2)
            at = (pl.ds(pl.multiple_of(block * batch, batch), batch), half_of)
            return pltpu.make_async_copy(
                waves_hbm.at[at], stage_ref.at[at], load_sem.at[2 + panels + step]
            )

        for step in range(2 * blocks):
            wave_copy(step).start()
    else:
        wave_copy = load(waves_hbm, waves_ref, 2 + panels)
    late_copies = [
        load(chirp_hbm.at[:, me_p], chirp_ref, 0),
        load(table_hbm, table_ref, 1),
    ]
    for copy in trial_copies:
        copy.wait()

    def lower_modes(row, carry):
        fields = jnp.concatenate(
            [trial_ref[b, pl.ds(row, order, stride=rows), :] for b in range(panels)], axis=1
        ).astype(jnp.bfloat16)
        at = pl.ds(pl.multiple_of(row * cols, 128), cols)
        low_ref[0, :, at] = fields
        low_ref[1, :, at] = jnp.concatenate([-fields[modes:], fields[:modes]], axis=0)
        return carry

    lax.fori_loop(0, rows, lower_modes, 0)

    def wave(half_of, row, count):
        return jnp.concatenate([waves_ref[half_of * rows + row + i] for i in range(count)], axis=1)

    def correlate(fields, row):
        swapped = jnp.concatenate([-fields[modes:], fields[:modes]], axis=0)
        rows_a[:, 0:electrons] += dot(fields, wave(0, row, lines), NT) + dot(
            swapped, wave(1, row, lines), NT
        )

    if raw:
        tile = band * 32
        pick_row = lax.broadcasted_iota(jnp.int32, (tile, tile), 0)
        pick_col = lax.broadcasted_iota(jnp.int32, (tile, tile), 1)
        pick_ref[...] = jnp.where(
            pick_col == lax.rem(pick_row, 32) * band + pick_row // 32, 1.0, 0.0
        ).astype(jnp.bfloat16)

        def sort_block(step, carry):
            wave_copy(step).wait()
            block, half_of = step // 2, lax.rem(step, 2)
            base = pl.multiple_of(block * batch, batch)

            def sort_band(band_of, carry):
                sorted_tiles = []
                for t in range(batch // 32):
                    mixed = stage_ref[pl.ds(base + t * 32, 32), half_of, band_of]
                    sorted_tiles.append(
                        dot(pick_ref[...], mixed.reshape(tile, cols), NN).astype(jnp.bfloat16)
                    )
                by_row = []
                for r in range(band):
                    row_wave = jnp.concatenate(
                        [value[r * 32 : (r + 1) * 32] for value in sorted_tiles], axis=0
                    )
                    waves_ref[half_of * rows + band_of * band + r, pl.ds(base, batch), :] = row_wave
                    by_row.append(row_wave)
                fields = low_ref[
                    half_of, :, pl.ds(pl.multiple_of(band_of * band * cols, 128), band * cols)
                ]
                rows_a[:, pl.ds(base, batch)] += dot(
                    fields, jnp.concatenate(by_row, axis=1), NT
                )
                return carry

            lax.fori_loop(0, rows // band, sort_band, 0)
            return carry

        lax.fori_loop(0, 2 * blocks, sort_block, 0)
    else:
        wave_copy.wait()

        def opening(step, carry):
            at = pl.ds(pl.multiple_of(step * sub, 128), sub)
            correlate(low_ref[0, :, at], step * lines)
            return carry

        lax.fori_loop(0, rows // lines, opening, 0)
    for copy in late_copies:
        copy.wait()
    for j in range(np_):
        part_ref[j] = rows_a[pl.ds(j * depth, depth), 0:electrons]
    pl.semaphore_wait(pltpu.get_barrier_semaphore(), greeted)
    started = scatter_gather(
        np_, peers, part_ref, held_a, total_a, ps.at[0], ps.at[1], ps.at[2], ps.at[3]
    )
    for j in range(np_):
        rows_a[pl.ds(j * depth, depth), 0:electrons] = total_a[j]

    def split_rows(value):
        upper = value.astype(jnp.bfloat16)
        both_ref[0:order, :] = upper
        both_ref[order : 2 * order, :] = (value - upper.astype(jnp.float32)).astype(jnp.bfloat16)

    def part(ref, lead, piece):
        return ref.at[lead, :, pl.ds(piece * width, width)]

    def cut(piece):
        return pl.ds(piece * width, width)

    def round_trip(turn, gathered, finish, beside):
        sa, ra, sb, rb, sc, rc, sd, rd, se, re = [es.at[10 * turn + i] for i in range(10)]
        first, second = {}, {}

        def compute(piece):
            def body(step, carry):
                start = pl.multiple_of(piece * width + step * sub, 128)
                row = (piece * (width // sub) + step) * lines
                both = both_ref[...]
                from_re = dot(both, wave(0, row, lines), NN)
                from_im = dot(both, wave(1, row, lines), NN)
                from_re = from_re[:order] + from_re[order:]
                from_im = from_im[:order] + from_im[order:]
                real = from_re[:modes] + from_im[modes:]
                imag = from_re[modes:] - from_im[:modes]
                if chunk % 16 == 0:
                    whole = jnp.concatenate([real, imag], axis=0).astype(jnp.bfloat16)
                    for j in range(ne):
                        x_ref[turn, j, :, pl.ds(start, sub)] = whole[j * chunk : (j + 1) * chunk]
                else:
                    cut_ref[0:modes, :] = real
                    cut_ref[modes:order, :] = imag
                    for j in range(ne):
                        x_ref[turn, j, :, pl.ds(start, sub)] = cut_ref[
                            pl.ds(j * chunk, chunk), :
                        ].astype(jnp.bfloat16)
                return carry

            lax.fori_loop(0, width // sub, body, 0)
            for d, other in enumerate(others + [chip]):
                slot = d * pieces + piece
                copy = remote(
                    part(x_ref.at[turn], other * 2 + 1 - core, piece),
                    part(pair.at[turn], d, piece),
                    sa.at[slot], ra.at[slot], "elec", partner,
                )
                copy.start()
                started.append(copy)
                first[d, piece] = copy

        def cross(piece):
            for d in range(chips - 1):
                slot = d * pieces + piece
                first[d, piece].wait_recv()
                half[turn, d, :, cut(piece)] = (
                    x_ref[turn, seats[d], :, cut(piece)].astype(jnp.float32)
                    + pair[turn, d, :, cut(piece)].astype(jnp.float32)
                ).astype(jnp.bfloat16)
                copy = remote(
                    part(half.at[turn], d, piece), part(far.at[turn], d, piece),
                    sb.at[slot], rb.at[slot], "elec", seats[d],
                )
                copy.start()
                started.append(copy)
                second[d, piece] = copy

        def close(piece):
            first[chips - 1, piece].wait_recv()
            total = x_ref[turn, me, :, cut(piece)].astype(jnp.float32) + pair[
                turn, chips - 1, :, cut(piece)
            ].astype(jnp.float32)
            for d in range(chips - 1):
                second[d, piece].wait_recv()
                total = total + far[turn, d, :, cut(piece)].astype(jnp.float32)
            gathered[me, :, cut(piece)] = total.astype(jnp.bfloat16)
            block = part(gathered, me, piece)
            for d in range(chips - 1):
                slot = d * pieces + piece
                copy = remote(block, block, sc.at[slot], rc.at[slot], "elec", seats[d])
                copy.start()
                started.append(copy)
            copy = remote(block, block, sd.at[piece], rd.at[piece], "elec", partner)
            copy.start()
            started.append(copy)

        def relay(piece):
            for d in range(chips - 1):
                slot = d * pieces + piece
                source = sources[d] * 2 + core
                block = part(gathered, source, piece)
                remote(block, block, sc.at[slot], rc.at[slot], "elec", source).wait_recv()
                copy = remote(block, block, se.at[slot], re.at[slot], "elec", partner)
                copy.start()
                started.append(copy)

        def arrive(piece):
            block = part(gathered, partner, piece)
            remote(block, block, sd.at[piece], rd.at[piece], "elec", partner).wait_recv()
            for d in range(chips - 1):
                slot = d * pieces + piece
                block = part(gathered, sources[d] * 2 + 1 - core, piece)
                remote(block, block, se.at[slot], re.at[slot], "elec", partner).wait_recv()
            finish(piece)

        for tick in range(pieces + 5):
            for lag, stage in ((0, compute), (1, cross), (3, close), (4, relay), (5, arrive)):
                if 0 <= tick - lag < pieces:
                    stage(tick - lag)
            if tick == pieces:
                beside()

    def stacked(gathered, start):
        if chunk % 16 == 0:
            return jnp.concatenate([gathered[j, :, pl.ds(start, sub)] for j in range(ne)], axis=0)
        for j in range(ne):
            cut_ref[pl.ds(j * chunk, chunk), :] = gathered[j, :, pl.ds(start, sub)].astype(
                jnp.float32
            )
        return cut_ref[...].astype(jnp.bfloat16)

    split_rows(rows_a[:, 0:electrons])
    rows_a[...] = jnp.zeros_like(rows_a)

    def project_piece(piece):
        def body(step, carry):
            start = pl.multiple_of(piece * width + step * sub, 128)
            fields = stacked(first_ref, start)
            correlate(fields, (piece * (width // sub) + step) * lines)
            rows_a[:, electrons : electrons + order] += dot(fields, fields, NT)
            return carry

        lax.fori_loop(0, width // sub, body, 0)

    round_trip(0, first_ref, project_piece, lambda: None)
    for j in range(np_):
        pay_ref[j] = rows_a[pl.ds(j * depth, depth), :]
    started += scatter_gather(
        np_, peers, pay_ref, held_b, total_b, ps.at[4], ps.at[5], ps.at[6], ps.at[7]
    )
    for j in range(np_):
        rows_a[pl.ds(j * depth, depth), :] = total_b[j]

    row_id = lax.broadcasted_iota(jnp.int32, (order, order), 0)
    col_id = lax.broadcasted_iota(jnp.int32, (order, order), 1)
    raw = rows_a[:, electrons : electrons + order]
    trace = 2.0 * jnp.sum(
        jnp.sum(jnp.where(row_id == col_id, raw, 0.0), axis=1, keepdims=True), axis=0, keepdims=True
    )
    split_rows(rows_a[:, 0:electrons] / jnp.sqrt(trace))

    def first_turn():
        gram_re = raw[:modes, :modes] + raw[modes:, modes:]
        gram_im = raw[:modes, modes:] - raw[modes:, :modes]
        emb_ref[0:modes, 0:modes] = gram_re
        emb_ref[0:modes, modes:order] = -gram_im
        emb_ref[modes:order, 0:modes] = gram_im
        emb_ref[modes:order, modes:order] = gram_re
        identity = jnp.where(row_id == col_id, 1.0, 0.0).astype(jnp.float32)
        turn_ref[...] = newton_schulz(emb_ref[...] / trace, identity)

    emb2 = [jnp.zeros((order, order), jnp.float32)]

    def gram_piece(piece):
        def body(step, carry):
            fields = stacked(applied_ref, pl.multiple_of(piece * width + step * sub, 128))
            return carry + dot(fields, fields, NT)

        emb2[0] = lax.fori_loop(0, width // sub, body, emb2[0])

    round_trip(1, applied_ref, gram_piece, first_turn)
    raw2 = emb2[0]
    gram_re = raw2[:modes, :modes] + raw2[modes:, modes:]
    gram_im = raw2[:modes, modes:] - raw2[modes:, :modes]
    low = modes // 2
    emb_ref[0:modes, 0:modes] = gram_re
    emb_ref[0:modes, modes:order] = gram_im
    gram_in[0, :, 0:order] = emb_ref[0:low, 0:order]
    gram_in[0, :, order : 2 * order] = emb_ref[low:modes, 0:order]
    last = []
    for d in range(1, np_):
        copy = remote(
            gram_in.at[0], gram_in.at[d], gs.at[0, d], gs.at[1, d], "pix", peers[d - 1]
        )
        copy.start()
        last.append(copy)
    total = gram_in[0]
    for d in range(1, np_):
        last[d - 1].wait_recv()
        total = total + gram_in[d]
    emb_ref[0:low, 0:order] = total[:, 0:order]
    emb_ref[low:modes, 0:order] = total[:, order : 2 * order]
    gram_re = emb_ref[0:modes, 0:modes]
    gram_im = emb_ref[0:modes, modes:order]
    emb_ref[0:modes, modes:order] = gram_im
    emb_ref[modes:order, 0:modes] = -gram_im
    emb_ref[modes:order, modes:order] = gram_re
    first_root = turn_ref[...]
    first_t = first_root.T
    raw = 0.5 * jnp.dot(
        jnp.dot(first_t, emb_ref[...], precision=HIGH), first_root, precision=HIGH
    )
    gram_re = raw[:modes, :modes] + raw[modes:, modes:]
    gram_im = raw[:modes, modes:] - raw[modes:, :modes]
    emb_ref[0:modes, 0:modes] = gram_re
    emb_ref[0:modes, modes:order] = -gram_im
    emb_ref[modes:order, 0:modes] = gram_im
    emb_ref[modes:order, modes:order] = gram_re
    embedded = emb_ref[...]
    diagonal = row_id == col_id
    trace = jnp.sum(
        jnp.sum(jnp.where(diagonal, embedded, 0.0), axis=1, keepdims=True), axis=0, keepdims=True
    )
    identity = jnp.where(diagonal, 1.0, 0.0).astype(jnp.float32)
    second_root = newton_schulz(embedded / trace, identity) / jnp.sqrt(trace)
    turn_ref[...] = jnp.dot(second_root.T, first_t, precision=HIGH)
    for part_of in range(2):
        emb_ref[pl.ds(part_of * share, share), :] = turn_ref[
            pl.ds(part_of * modes + me * share, share), :
        ]
    mine = emb_ref[0 : 2 * share, :]
    upper = mine.astype(jnp.bfloat16)
    lower = (mine - upper.astype(jnp.float32)).astype(jnp.bfloat16)
    group = next(count for count in (8, 5, 4, 2, 1) if rows % count == 0)

    def rotate(step, carry):
        start = pl.multiple_of(step * (group * cols), 128)
        if chunk % 16 == 0:
            fields = jnp.concatenate(
                [applied_ref[j, :, pl.ds(start, group * cols)] for j in range(ne)], axis=0
            )
        else:
            fields = jnp.concatenate(
                [
                    applied_ref[j, :, pl.ds(start, group * cols)].astype(jnp.float32)
                    for j in range(ne)
                ],
                axis=0,
            ).astype(jnp.bfloat16)
        turned = dot(upper, fields, NN) + dot(lower, fields, NN)
        for i in range(group):
            for b in range(cols // 128):
                lines_ref[b, pl.ds((step * group + i) * 2 * share, 2 * share), :] = turned[
                    :, i * cols + b * 128 : i * cols + (b + 1) * 128
                ]
        return carry

    lax.fori_loop(0, rows // group, rotate, 0)
    chirp_re, chirp_im = chirp_ref[0], chirp_ref[1]
    for m in range(share):
        real = jnp.concatenate(
            [lines_ref[b, pl.ds(m, rows, stride=2 * share), :] for b in range(cols // 128)], axis=1
        )
        imag = jnp.concatenate(
            [
                lines_ref[b, pl.ds(share + m, rows, stride=2 * share), :]
                for b in range(cols // 128)
            ],
            axis=1,
        )
        launch_ref[m * rows : (m + 1) * rows, 0:cols] = chirp_re * real - chirp_im * imag
        launch_ref[m * rows : (m + 1) * rows, cols : 2 * cols] = chirp_re * imag + chirp_im * real
    launch = launch_ref[...]
    upper = launch.astype(jnp.bfloat16)
    lower = (launch - upper.astype(jnp.float32)).astype(jnp.bfloat16)
    spec_ref[...] = (
        dot(upper, table_ref[0], NN) + dot(upper, table_ref[1], NN) + dot(lower, table_ref[0], NN)
    )
    thin = cols // np_
    for p in range(np_):
        for c in range(2):
            for m in range(share):
                at = (2 * p + c) * thin
                to = (c * share + m) * thin
                send_ref[p, :, to : to + thin] = spec_ref[
                    m * rows : (m + 1) * rows, at : at + thin
                ].astype(jnp.bfloat16)
    swaps = []
    for d in range(1, np_):
        copy = remote(
            send_ref.at[peers[d - 1]], out_ref.at[me_p], gs.at[2, d], gs.at[3, d], "pix",
            peers[d - 1],
        )
        copy.start()
        swaps.append(copy)
    out_ref[me_p] = send_ref[me_p]
    for d in range(1, np_):
        source = lax.rem(me_p + np_ - d, np_)
        block = out_ref.at[source]
        remote(block, block, gs.at[2, d], gs.at[3, d], "pix", source).wait_recv()
    for copy in started + last + swaps:
        copy.wait_send()


def middle(waves, trial, chirp, tables):
    np_ = lax.axis_size("pix")
    ne = lax.axis_size("elec")
    electrons, _, rows, cols = waves.shape
    mode_count = trial.shape[1]
    pixels = rows * cols
    order = 2 * mode_count
    chunk = order // ne
    depth = order // np_
    raw = rows % 8 == 0 and electrons % EBLOCK == 0
    if raw:
        waves = waves.reshape(electrons, 2, rows // 8, 8, cols)
        stage = waves.shape
    else:
        waves = waves.transpose(1, 2, 0, 3).reshape(2 * rows, electrons, cols)
        stage = (1, 1, 1, 8, 128)
    trial = trial.reshape(order * rows, cols)
    pieces = next(count for count in (4, 2, 1) if rows % count == 0)
    lines = next(size for size in (5, 4, 2, 1) if rows // pieces % size == 0)
    sub = lines * cols
    chips = ne // 2
    wide = electrons + order + -order % 128
    share = mode_count // ne
    lanes = 2 * share * (cols // np_)
    vmem = pl.BlockSpec(memory_space=pltpu.VMEM)
    hbm = pl.BlockSpec(memory_space=pl.ANY)
    dma = pltpu.SemaphoreType.DMA
    f32, bf16 = jnp.float32, jnp.bfloat16
    return pl.pallas_call(
        functools.partial(core_kernel, np_, ne, pieces, sub, electrons, mode_count, raw),
        out_shape=jax.ShapeDtypeStruct((np_, rows, lanes), bf16),
        in_specs=[hbm] * 4,
        out_specs=vmem,
        scratch_shapes=[
            pltpu.VMEM(stage, bf16),
            pltpu.VMEM((2 * rows, electrons, cols), bf16),
            pltpu.VMEM((cols // 128, order * rows, 128), f32),
            pltpu.VMEM((2, order, pixels), bf16),
            pltpu.VMEM((2, rows, cols), f32),
            pltpu.VMEM(tables.shape, bf16),
            pltpu.VMEM((256, 256), bf16),
            pltpu.VMEM((ne, chunk, pixels), bf16),
            pltpu.VMEM((order, order), f32),
            pltpu.VMEM((np_, depth, electrons), f32),
            pltpu.VMEM((cols // 128, rows * 2 * share, 128), f32),
            pltpu.VMEM((share * rows, 2 * cols), f32),
            pltpu.VMEM((share * rows, 2 * cols), f32),
            pltpu.VMEM((np_, rows, lanes), bf16),
            pltpu.VMEM((order, wide), f32),
            pltpu.VMEM((2 * order, electrons), bf16),
            pltpu.VMEM((order, sub), f32),
            pltpu.VMEM((order, order), f32),
            pltpu.VMEM((np_, depth, electrons), f32),
            pltpu.VMEM((np_, depth, electrons), f32),
            pltpu.VMEM((np_, depth, wide), f32),
            pltpu.VMEM((np_, depth, wide), f32),
            pltpu.VMEM((np_, depth, wide), f32),
            pltpu.VMEM((2, ne, chunk, pixels), bf16),
            pltpu.VMEM((2, chips, chunk, pixels), bf16),
            pltpu.VMEM((2, chips, chunk, pixels), bf16),
            pltpu.VMEM((2, chips, chunk, pixels), bf16),
            pltpu.VMEM((ne, chunk, pixels), bf16),
            pltpu.VMEM((np_, mode_count // 2, 2 * order), f32),
            dma((8, np_)),
            dma((20, chips * pieces)),
            dma((4, np_)),
            dma((2 + cols // 128 + max(1, 2 * electrons // EBLOCK),)),
        ],
        compiler_params=pltpu.CompilerParams(
            collective_id=1, has_side_effects=True, vmem_limit_bytes=60 * 1024 * 1024
        ),
        name="middle",
    )(waves, trial, chirp, tables)


def newton_schulz(scaled, identity):
    inverse_root = identity
    for step in range(NS_STEPS):
        product = scaled if step == 0 else jnp.dot(inverse_root, scaled, precision=HIGH)
        correction = 1.5 * identity - 0.5 * product
        if step == 0:
            inverse_root = correction
        else:
            inverse_root = jnp.dot(correction, inverse_root, precision=HIGH)
        if step + 1 < NS_STEPS:
            scaled = jnp.dot(scaled, correction, precision=HIGH)
    return inverse_root


def dft_table(length):
    index = np.arange(length, dtype=np.int64)
    angle = 2.0 * np.pi / length * (index[:, None] * index[None, :] % length)
    return np.cos(angle).astype(np.float32), -np.sin(angle).astype(np.float32)


def split(table):
    upper = table.astype(jnp.bfloat16)
    lower = (table - upper.astype(np.float32)).astype(jnp.bfloat16)
    return upper, lower


def chirp_phase(row_pos, col_pos, row_total, col_total, factor):
    row_term = (row_pos - row_total / 2.0) ** 2 / row_total
    col_term = (col_pos - col_total / 2.0) ** 2 / col_total
    angle = math.pi * factor * (row_term[:, None] + col_term[None, :])
    return (jnp.cos(angle), jnp.sin(angle))


def column_tables(length, pix_count):
    table_re, table_im = dft_table(length)
    full = np.stack([np.stack([table_re, table_im], 1), np.stack([-table_im, table_re], 1)])
    full = full.reshape(2, length, 2, pix_count, length // pix_count).transpose(0, 1, 3, 2, 4)
    return np.stack(split(full.reshape(2 * length, 2 * length)))


def row_section(spectrum, share, col_pos, row_total, col_total):
    width = col_pos.shape[0]
    table_re, table_im = dft_table(row_total)
    upper, lower = split(np.concatenate([table_re, table_im], axis=0))
    tables = np.concatenate([upper, lower], axis=0)
    wide = jnp.dot(jnp.asarray(tables), spectrum, preferred_element_type=jnp.float32)
    wide = wide[: 2 * row_total] + wide[2 * row_total :]
    half = share * width
    out_re = wide[:row_total, :half] - wide[row_total:, half:]
    out_im = wide[:row_total, half:] + wide[row_total:, :half]
    row_pos = jnp.arange(row_total, dtype=jnp.float32)
    chirp_re, chirp_im = chirp_phase(row_pos, col_pos, row_total, col_total, 0.25)
    out_re = out_re.reshape(row_total, share, width).transpose(1, 0, 2)
    out_im = out_im.reshape(row_total, share, width).transpose(1, 0, 2)
    return jnp.stack([chirp_re * out_re - chirp_im * out_im, chirp_re * out_im + chirp_im * out_re])


def launch_chirp(row_total, cols):
    row_term = (np.arange(row_total) - row_total / 2.0) ** 2 / row_total
    col_term = (np.arange(cols) - cols / 2.0) ** 2 / cols
    angle = math.pi * 0.5 * (row_term[:, None] + col_term[None, :])
    return np.stack([np.cos(angle), np.sin(angle)]).astype(np.float32)


def shards(wavefronts, trial_modes):
    rows_dev, cols = wavefronts.shape[2:]
    share = trial_modes.shape[1] // lax.axis_size("elec")
    pix_count = lax.axis_size("pix")
    row_total = rows_dev * pix_count
    chirp = jnp.asarray(launch_chirp(row_total, cols).reshape(2, pix_count, rows_dev, cols))
    tables = jnp.asarray(column_tables(cols, pix_count))
    column_block = middle(wavefronts, trial_modes, chirp, tables).reshape(row_total, -1)
    width = cols // pix_count
    col_pos = (lax.axis_index("pix") * width + jnp.arange(width, dtype=jnp.int32)).astype(
        jnp.float32
    )
    return row_section(column_block, share, col_pos, row_total, cols)


def solution(mesh):
    in_specs = (P("elec", None, "pix", None), P(None, None, "pix", None))
    out_specs = P(None, "elec", None, "pix")
    return jax.shard_map(shards, mesh=mesh, in_specs=in_specs, out_specs=out_specs, check_vma=False)
```

```python
import functools
import math

import jax
import jax.numpy as jnp
import numpy as np
from jax import lax
from jax.experimental import pallas as pl
from jax.experimental.pallas import tpu as pltpu
from jax.sharding import PartitionSpec as P

NS_STEPS = 8

HIGH = lax.Precision.HIGHEST
MESH = pl.DeviceIdType.MESH
EBLOCK = 128


def greet(*groups):
    barrier = pltpu.get_barrier_semaphore()
    for axis, peers in groups:
        for peer in peers:
            pl.semaphore_signal(barrier, inc=1, device_id={axis: peer}, device_id_type=MESH)
    return sum(len(peers) for _, peers in groups)


def remote(src, dst, send_sem, recv_sem, axis, peer):
    return pltpu.make_async_remote_copy(
        src_ref=src,
        dst_ref=dst,
        send_sem=send_sem,
        recv_sem=recv_sem,
        device_id={axis: peer},
        device_id_type=MESH,
    )


NT = (((1,), (1,)), ((), ()))
NN = (((1,), (0,)), ((), ()))


def dot(left, right, dims):
    return lax.dot_general(left, right, dims, preferred_element_type=jnp.float32)


def scatter_gather(n, peers, x_ref, held, out_ref, send_a, recv_a, send_b, recv_b):
    me = lax.axis_index("pix")
    started = []
    scatter = []
    for d in range(1, n):
        peer = peers[d - 1]
        copy = remote(x_ref.at[peer], held.at[d], send_a.at[d], recv_a.at[d], "pix", peer)
        copy.start()
        scatter.append(copy)
    total = x_ref[me]
    for d in range(1, n):
        scatter[d - 1].wait_recv()
        total = total + held[d]
    out_ref[me] = total
    for d in range(1, n):
        copy = remote(
            out_ref.at[me], out_ref.at[me], send_b.at[d], recv_b.at[d], "pix", peers[d - 1]
        )
        copy.start()
        started.append(copy)
    for d in range(1, n):
        source = lax.rem(me + n - d, n)
        block = out_ref.at[source]
        remote(block, block, send_b.at[d], recv_b.at[d], "pix", source).wait_recv()
    return scatter + started


def core_kernel(
    np_, ne, pieces, sub, electrons, modes, raw,
    waves_hbm, trial_hbm, table_hbm,
    out_ref,
    stage_ref, waves_ref, trial_ref, low_ref, chirp_ref, table_ref, pick_ref,
    applied_ref, turn_ref, part_ref, lines_ref, launch_ref, spec_ref, send_ref, rows_a, both_ref, cut_ref, emb_ref,
    held_a, total_a, pay_ref, held_b, total_b,
    x_ref, pair, half, far, first_ref, gram_in,
    ps, es, gs, load_sem,
):
    share = modes // ne
    rows, cols = chirp_ref.shape[1:]
    pixels = rows * cols
    lines = sub // cols
    order = 2 * modes
    chunk = order // ne
    depth = order // np_
    width = pixels // pieces
    me_p = lax.axis_index("pix")
    peers = [lax.rem(me_p + d, np_) for d in range(1, np_)]
    me = lax.axis_index("elec")
    core = lax.rem(me, 2)
    chip = me // 2
    chips = ne // 2
    partner = chip * 2 + 1 - core
    others = [lax.rem(chip + d, chips) for d in range(1, chips)]
    seats = [other * 2 + core for other in others]
    sources = [lax.rem(chip + chips - d, chips) for d in range(1, chips)]
    greeted = greet(("pix", peers), ("elec", [partner] + seats))
    rows_a[...] = jnp.zeros_like(rows_a)

    def load(src, dst, slot):
        copy = pltpu.make_async_copy(src, dst, load_sem.at[slot])
        copy.start()
        return copy

    panels = cols // 128
    trial_copies = [
        load(trial_hbm.at[:, pl.ds(b * 128, 128)], trial_ref.at[b], 2 + b) for b in range(panels)
    ]
    if raw:
        band, batch = 8, EBLOCK
        blocks = electrons // batch

        def wave_copy(step):
            block, half_of = step // 2, lax.rem(step, 2)
            at = (pl.ds(pl.multiple_of(block * batch, batch), batch), half_of)
            return pltpu.make_async_copy(
                waves_hbm.at[at], stage_ref.at[at], load_sem.at[2 + panels + step]
            )

        for step in range(2 * blocks):
            wave_copy(step).start()
    else:
        wave_copy = load(waves_hbm, waves_ref, 2 + panels)
    table_copy = load(table_hbm, table_ref, 1)
    row_pos = (lax.broadcasted_iota(jnp.int32, (rows, 128), 0) + me_p * rows).astype(jnp.float32)
    col_pos = lax.broadcasted_iota(jnp.int32, (8, cols), 1).astype(jnp.float32)
    row_all = float(rows * np_)
    row_angle = (math.pi * 0.5) * (row_pos - row_all / 2.0) ** 2 / row_all
    col_angle = (math.pi * 0.5) * (col_pos - cols / 2.0) ** 2 / float(cols)
    row_cos, row_sin = jnp.cos(row_angle)[:, 0:1], jnp.sin(row_angle)[:, 0:1]
    col_cos, col_sin = jnp.cos(col_angle)[0:1], jnp.sin(col_angle)[0:1]
    chirp_ref[0] = row_cos * col_cos - row_sin * col_sin
    chirp_ref[1] = row_sin * col_cos + row_cos * col_sin
    for copy in trial_copies:
        copy.wait()

    def lower_modes(row, carry):
        fields = jnp.concatenate(
            [trial_ref[b, pl.ds(row, order, stride=rows), :] for b in range(panels)], axis=1
        ).astype(jnp.bfloat16)
        at = pl.ds(pl.multiple_of(row * cols, 128), cols)
        low_ref[:, at] = fields
        return carry

    lax.fori_loop(0, rows, lower_modes, 0)

    def wave(half_of, row, count):
        return jnp.concatenate([waves_ref[half_of * rows + row + i] for i in range(count)], axis=1)

    def correlate(fields, row):
        swapped = jnp.concatenate([-fields[modes:], fields[:modes]], axis=0)
        rows_a[:, 0:electrons] += dot(fields, wave(0, row, lines), NT) + dot(
            swapped, wave(1, row, lines), NT
        )

    if raw:
        tile = band * 32
        pick_row = lax.broadcasted_iota(jnp.int32, (tile, tile), 0)
        pick_col = lax.broadcasted_iota(jnp.int32, (tile, tile), 1)
        pick_ref[...] = jnp.where(
            pick_col == lax.rem(pick_row, 32) * band + pick_row // 32, 1.0, 0.0
        ).astype(jnp.bfloat16)

        def sort_block(step, carry):
            wave_copy(step).wait()
            block, half_of = step // 2, lax.rem(step, 2)
            base = pl.multiple_of(block * batch, batch)

            for band_of in range(rows // band):
                sorted_tiles = []
                for t in range(batch // 32):
                    mixed = stage_ref[pl.ds(base + t * 32, 32), half_of, band_of]
                    sorted_tiles.append(
                        dot(pick_ref[...], mixed.reshape(tile, cols), NN).astype(jnp.bfloat16)
                    )
                for r in range(band):
                    for t in range(batch // 32):
                        waves_ref[
                            half_of * rows + band_of * band + r, pl.ds(base + t * 32, 32), :
                        ] = sorted_tiles[t][r * 32 : (r + 1) * 32]
            return carry

        lax.fori_loop(0, 2 * blocks, sort_block, 0)
    else:
        wave_copy.wait()

    def opening(step, carry):
        at = pl.ds(pl.multiple_of(step * sub, 128), sub)
        correlate(low_ref[:, at], step * lines)
        return carry

    lax.fori_loop(0, rows // lines, opening, 0)
    table_copy.wait()
    for j in range(np_):
        part_ref[j] = rows_a[pl.ds(j * depth, depth), 0:electrons]
    pl.semaphore_wait(pltpu.get_barrier_semaphore(), greeted)
    started = scatter_gather(
        np_, peers, part_ref, held_a, total_a, ps.at[0], ps.at[1], ps.at[2], ps.at[3]
    )
    for j in range(np_):
        rows_a[pl.ds(j * depth, depth), 0:electrons] = total_a[j]

    def split_rows(value):
        upper = value.astype(jnp.bfloat16)
        both_ref[0:order, :] = upper
        both_ref[order : 2 * order, :] = (value - upper.astype(jnp.float32)).astype(jnp.bfloat16)

    def part(ref, lead, piece):
        return ref.at[lead, :, pl.ds(piece * width, width)]

    def cut(piece):
        return pl.ds(piece * width, width)

    def round_trip(turn, gathered, finish, beside):
        sa, ra, sb, rb, sc, rc, sd, rd, se, re = [es.at[10 * turn + i] for i in range(10)]
        first, second = {}, {}

        def compute(piece):
            def body(step, carry):
                start = pl.multiple_of(piece * width + step * sub, 128)
                row = (piece * (width // sub) + step) * lines
                both = both_ref[...]
                from_re = dot(both, wave(0, row, lines), NN)
                from_im = dot(both, wave(1, row, lines), NN)
                from_re = from_re[:order] + from_re[order:]
                from_im = from_im[:order] + from_im[order:]
                real = from_re[:modes] + from_im[modes:]
                imag = from_re[modes:] - from_im[:modes]
                if chunk % 16 == 0:
                    whole = jnp.concatenate([real, imag], axis=0).astype(jnp.bfloat16)
                    for j in range(ne):
                        x_ref[turn, j, :, pl.ds(start, sub)] = whole[j * chunk : (j + 1) * chunk]
                else:
                    cut_ref[0:modes, :] = real
                    cut_ref[modes:order, :] = imag
                    for j in range(ne):
                        x_ref[turn, j, :, pl.ds(start, sub)] = cut_ref[
                            pl.ds(j * chunk, chunk), :
                        ].astype(jnp.bfloat16)
                return carry

            lax.fori_loop(0, width // sub, body, 0)
            for d, other in enumerate(others + [chip]):
                slot = d * pieces + piece
                copy = remote(
                    part(x_ref.at[turn], other * 2 + 1 - core, piece),
                    part(pair.at[turn], d, piece),
                    sa.at[slot], ra.at[slot], "elec", partner,
                )
                copy.start()
                started.append(copy)
                first[d, piece] = copy

        def cross(piece):
            for d in range(chips - 1):
                slot = d * pieces + piece
                first[d, piece].wait_recv()
                half[turn, d, :, cut(piece)] = (
                    x_ref[turn, seats[d], :, cut(piece)].astype(jnp.float32)
                    + pair[turn, d, :, cut(piece)].astype(jnp.float32)
                ).astype(jnp.bfloat16)
                copy = remote(
                    part(half.at[turn], d, piece), part(far.at[turn], d, piece),
                    sb.at[slot], rb.at[slot], "elec", seats[d],
                )
                copy.start()
                started.append(copy)
                second[d, piece] = copy

        def close(piece):
            first[chips - 1, piece].wait_recv()
            total = x_ref[turn, me, :, cut(piece)].astype(jnp.float32) + pair[
                turn, chips - 1, :, cut(piece)
            ].astype(jnp.float32)
            for d in range(chips - 1):
                second[d, piece].wait_recv()
                total = total + far[turn, d, :, cut(piece)].astype(jnp.float32)
            gathered[me, :, cut(piece)] = total.astype(jnp.bfloat16)
            block = part(gathered, me, piece)
            for d in range(chips - 1):
                slot = d * pieces + piece
                copy = remote(block, block, sc.at[slot], rc.at[slot], "elec", seats[d])
                copy.start()
                started.append(copy)
            copy = remote(block, block, sd.at[piece], rd.at[piece], "elec", partner)
            copy.start()
            started.append(copy)

        def relay(piece):
            for d in range(chips - 1):
                slot = d * pieces + piece
                source = sources[d] * 2 + core
                block = part(gathered, source, piece)
                remote(block, block, sc.at[slot], rc.at[slot], "elec", source).wait_recv()
                copy = remote(block, block, se.at[slot], re.at[slot], "elec", partner)
                copy.start()
                started.append(copy)

        def arrive(piece):
            block = part(gathered, partner, piece)
            remote(block, block, sd.at[piece], rd.at[piece], "elec", partner).wait_recv()
            for d in range(chips - 1):
                slot = d * pieces + piece
                block = part(gathered, sources[d] * 2 + 1 - core, piece)
                remote(block, block, se.at[slot], re.at[slot], "elec", partner).wait_recv()
            finish(piece)

        for tick in range(pieces + 5):
            for lag, stage in ((0, compute), (1, cross), (3, close), (4, relay), (5, arrive)):
                if 0 <= tick - lag < pieces:
                    stage(tick - lag)
            if tick == pieces:
                beside()

    def stacked(gathered, start):
        if chunk % 16 == 0:
            return jnp.concatenate([gathered[j, :, pl.ds(start, sub)] for j in range(ne)], axis=0)
        for j in range(ne):
            cut_ref[pl.ds(j * chunk, chunk), :] = gathered[j, :, pl.ds(start, sub)].astype(
                jnp.float32
            )
        return cut_ref[...].astype(jnp.bfloat16)

    split_rows(rows_a[:, 0:electrons])
    rows_a[...] = jnp.zeros_like(rows_a)

    def project_piece(piece):
        def body(step, carry):
            start = pl.multiple_of(piece * width + step * sub, 128)
            fields = stacked(first_ref, start)
            correlate(fields, (piece * (width // sub) + step) * lines)
            rows_a[:, electrons : electrons + order] += dot(fields, fields, NT)
            return carry

        lax.fori_loop(0, width // sub, body, 0)

    round_trip(0, first_ref, project_piece, lambda: None)
    for j in range(np_):
        pay_ref[j] = rows_a[pl.ds(j * depth, depth), :]
    started += scatter_gather(
        np_, peers, pay_ref, held_b, total_b, ps.at[4], ps.at[5], ps.at[6], ps.at[7]
    )
    for j in range(np_):
        rows_a[pl.ds(j * depth, depth), :] = total_b[j]

    row_id = lax.broadcasted_iota(jnp.int32, (order, order), 0)
    col_id = lax.broadcasted_iota(jnp.int32, (order, order), 1)
    raw = rows_a[:, electrons : electrons + order]
    trace = 2.0 * jnp.sum(
        jnp.sum(jnp.where(row_id == col_id, raw, 0.0), axis=1, keepdims=True), axis=0, keepdims=True
    )
    split_rows(rows_a[:, 0:electrons] / jnp.sqrt(trace))

    def first_turn():
        gram_re = raw[:modes, :modes] + raw[modes:, modes:]
        gram_im = raw[:modes, modes:] - raw[modes:, :modes]
        emb_ref[0:modes, 0:modes] = gram_re
        emb_ref[0:modes, modes:order] = -gram_im
        emb_ref[modes:order, 0:modes] = gram_im
        emb_ref[modes:order, modes:order] = gram_re
        identity = jnp.where(row_id == col_id, 1.0, 0.0).astype(jnp.float32)
        turn_ref[...] = newton_schulz(emb_ref[...] / trace, identity)

    emb2 = [jnp.zeros((order, order), jnp.float32)]

    def gram_piece(piece):
        def body(step, carry):
            fields = stacked(applied_ref, pl.multiple_of(piece * width + step * sub, 128))
            return carry + dot(fields, fields, NT)

        emb2[0] = lax.fori_loop(0, width // sub, body, emb2[0])

    round_trip(1, applied_ref, gram_piece, first_turn)
    raw2 = emb2[0]
    gram_re = raw2[:modes, :modes] + raw2[modes:, modes:]
    gram_im = raw2[:modes, modes:] - raw2[modes:, :modes]
    low = modes // 2
    emb_ref[0:modes, 0:modes] = gram_re
    emb_ref[0:modes, modes:order] = gram_im
    gram_in[0, :, 0:order] = emb_ref[0:low, 0:order]
    gram_in[0, :, order : 2 * order] = emb_ref[low:modes, 0:order]
    last = []
    for d in range(1, np_):
        copy = remote(
            gram_in.at[0], gram_in.at[d], gs.at[0, d], gs.at[1, d], "pix", peers[d - 1]
        )
        copy.start()
        last.append(copy)
    total = gram_in[0]
    for d in range(1, np_):
        last[d - 1].wait_recv()
        total = total + gram_in[d]
    emb_ref[0:low, 0:order] = total[:, 0:order]
    emb_ref[low:modes, 0:order] = total[:, order : 2 * order]
    gram_re = emb_ref[0:modes, 0:modes]
    gram_im = emb_ref[0:modes, modes:order]
    emb_ref[0:modes, modes:order] = gram_im
    emb_ref[modes:order, 0:modes] = -gram_im
    emb_ref[modes:order, modes:order] = gram_re
    first_root = turn_ref[...]
    first_t = first_root.T
    raw = 0.5 * jnp.dot(
        jnp.dot(first_t, emb_ref[...], precision=HIGH), first_root, precision=HIGH
    )
    gram_re = raw[:modes, :modes] + raw[modes:, modes:]
    gram_im = raw[:modes, modes:] - raw[modes:, :modes]
    emb_ref[0:modes, 0:modes] = gram_re
    emb_ref[0:modes, modes:order] = -gram_im
    emb_ref[modes:order, 0:modes] = gram_im
    emb_ref[modes:order, modes:order] = gram_re
    embedded = emb_ref[...]
    diagonal = row_id == col_id
    trace = jnp.sum(
        jnp.sum(jnp.where(diagonal, embedded, 0.0), axis=1, keepdims=True), axis=0, keepdims=True
    )
    identity = jnp.where(diagonal, 1.0, 0.0).astype(jnp.float32)
    second_root = newton_schulz(embedded / trace, identity) / jnp.sqrt(trace)
    turn_ref[...] = jnp.dot(second_root.T, first_t, precision=HIGH)
    for part_of in range(2):
        emb_ref[pl.ds(part_of * share, share), :] = turn_ref[
            pl.ds(part_of * modes + me * share, share), :
        ]
    mine = emb_ref[0 : 2 * share, :]
    upper = mine.astype(jnp.bfloat16)
    lower = (mine - upper.astype(jnp.float32)).astype(jnp.bfloat16)
    group = next(count for count in (8, 5, 4, 2, 1) if rows % count == 0)

    def rotate(step, carry):
        start = pl.multiple_of(step * (group * cols), 128)
        if chunk % 16 == 0:
            fields = jnp.concatenate(
                [applied_ref[j, :, pl.ds(start, group * cols)] for j in range(ne)], axis=0
            )
        else:
            fields = jnp.concatenate(
                [
                    applied_ref[j, :, pl.ds(start, group * cols)].astype(jnp.float32)
                    for j in range(ne)
                ],
                axis=0,
            ).astype(jnp.bfloat16)
        turned = dot(upper, fields, NN) + dot(lower, fields, NN)
        for i in range(group):
            for b in range(cols // 128):
                lines_ref[b, pl.ds((step * group + i) * 2 * share, 2 * share), :] = turned[
                    :, i * cols + b * 128 : i * cols + (b + 1) * 128
                ]
        return carry

    lax.fori_loop(0, rows // group, rotate, 0)
    chirp_re, chirp_im = chirp_ref[0], chirp_ref[1]
    for m in range(share):
        real = jnp.concatenate(
            [lines_ref[b, pl.ds(m, rows, stride=2 * share), :] for b in range(cols // 128)], axis=1
        )
        imag = jnp.concatenate(
            [
                lines_ref[b, pl.ds(share + m, rows, stride=2 * share), :]
                for b in range(cols // 128)
            ],
            axis=1,
        )
        launch_ref[m * rows : (m + 1) * rows, 0:cols] = chirp_re * real - chirp_im * imag
        launch_ref[m * rows : (m + 1) * rows, cols : 2 * cols] = chirp_re * imag + chirp_im * real
    launch = launch_ref[...]
    upper = launch.astype(jnp.bfloat16)
    lower = (launch - upper.astype(jnp.float32)).astype(jnp.bfloat16)
    spec_ref[...] = (
        dot(upper, table_ref[0], NN) + dot(upper, table_ref[1], NN) + dot(lower, table_ref[0], NN)
    )
    thin = cols // np_
    for p in range(np_):
        for c in range(2):
            for m in range(share):
                at = (2 * p + c) * thin
                to = (c * share + m) * thin
                send_ref[p, :, to : to + thin] = spec_ref[
                    m * rows : (m + 1) * rows, at : at + thin
                ].astype(jnp.bfloat16)
    swaps = []
    for d in range(1, np_):
        copy = remote(
            send_ref.at[peers[d - 1]], out_ref.at[me_p], gs.at[2, d], gs.at[3, d], "pix",
            peers[d - 1],
        )
        copy.start()
        swaps.append(copy)
    out_ref[me_p] = send_ref[me_p]
    for d in range(1, np_):
        source = lax.rem(me_p + np_ - d, np_)
        block = out_ref.at[source]
        remote(block, block, gs.at[2, d], gs.at[3, d], "pix", source).wait_recv()
    for copy in started + last + swaps:
        copy.wait_send()


def middle(waves, trial, tables):
    np_ = lax.axis_size("pix")
    ne = lax.axis_size("elec")
    electrons, _, rows, cols = waves.shape
    mode_count = trial.shape[1]
    pixels = rows * cols
    order = 2 * mode_count
    chunk = order // ne
    depth = order // np_
    raw = rows % 8 == 0 and electrons % EBLOCK == 0
    if raw:
        waves = waves.reshape(electrons, 2, rows // 8, 8, cols)
        stage = waves.shape
    else:
        waves = waves.transpose(1, 2, 0, 3).reshape(2 * rows, electrons, cols)
        stage = (1, 1, 1, 8, 128)
    trial = trial.reshape(order * rows, cols)
    pieces = next(count for count in (4, 2, 1) if rows % count == 0)
    lines = next(size for size in (5, 4, 2, 1) if rows // pieces % size == 0)
    sub = lines * cols
    chips = ne // 2
    wide = electrons + order + -order % 128
    share = mode_count // ne
    lanes = 2 * share * (cols // np_)
    vmem = pl.BlockSpec(memory_space=pltpu.VMEM)
    hbm = pl.BlockSpec(memory_space=pl.ANY)
    dma = pltpu.SemaphoreType.DMA
    f32, bf16 = jnp.float32, jnp.bfloat16
    return pl.pallas_call(
        functools.partial(core_kernel, np_, ne, pieces, sub, electrons, mode_count, raw),
        out_shape=jax.ShapeDtypeStruct((np_, rows, lanes), bf16),
        in_specs=[hbm] * 3,
        out_specs=vmem,
        scratch_shapes=[
            pltpu.VMEM(stage, bf16),
            pltpu.VMEM((2 * rows, electrons, cols), bf16),
            pltpu.VMEM((cols // 128, order * rows, 128), f32),
            pltpu.VMEM((order, pixels), bf16),
            pltpu.VMEM((2, rows, cols), f32),
            pltpu.VMEM(tables.shape, bf16),
            pltpu.VMEM((256, 256), bf16),
            pltpu.VMEM((ne, chunk, pixels), bf16),
            pltpu.VMEM((order, order), f32),
            pltpu.VMEM((np_, depth, electrons), f32),
            pltpu.VMEM((cols // 128, rows * 2 * share, 128), f32),
            pltpu.VMEM((share * rows, 2 * cols), f32),
            pltpu.VMEM((share * rows, 2 * cols), f32),
            pltpu.VMEM((np_, rows, lanes), bf16),
            pltpu.VMEM((order, wide), f32),
            pltpu.VMEM((2 * order, electrons), bf16),
            pltpu.VMEM((order, sub), f32),
            pltpu.VMEM((order, order), f32),
            pltpu.VMEM((np_, depth, electrons), f32),
            pltpu.VMEM((np_, depth, electrons), f32),
            pltpu.VMEM((np_, depth, wide), f32),
            pltpu.VMEM((np_, depth, wide), f32),
            pltpu.VMEM((np_, depth, wide), f32),
            pltpu.VMEM((2, ne, chunk, pixels), bf16),
            pltpu.VMEM((2, chips, chunk, pixels), bf16),
            pltpu.VMEM((2, chips, chunk, pixels), bf16),
            pltpu.VMEM((2, chips, chunk, pixels), bf16),
            pltpu.VMEM((ne, chunk, pixels), bf16),
            pltpu.VMEM((np_, mode_count // 2, 2 * order), f32),
            dma((8, np_)),
            dma((20, chips * pieces)),
            dma((4, np_)),
            dma((2 + cols // 128 + max(1, 2 * electrons // EBLOCK),)),
        ],
        compiler_params=pltpu.CompilerParams(
            collective_id=1, has_side_effects=True, vmem_limit_bytes=60 * 1024 * 1024
        ),
        name="middle",
    )(waves, trial, tables)


def newton_schulz(scaled, identity):
    inverse_root = identity
    for step in range(NS_STEPS):
        product = scaled if step == 0 else jnp.dot(inverse_root, scaled, precision=HIGH)
        correction = 1.5 * identity - 0.5 * product
        if step == 0:
            inverse_root = correction
        else:
            inverse_root = jnp.dot(correction, inverse_root, precision=HIGH)
        if step + 1 < NS_STEPS:
            scaled = jnp.dot(scaled, correction, precision=HIGH)
    return inverse_root


def dft_table(length):
    index = np.arange(length, dtype=np.int64)
    angle = 2.0 * np.pi / length * (index[:, None] * index[None, :] % length)
    return np.cos(angle).astype(np.float32), -np.sin(angle).astype(np.float32)


def split(table):
    upper = table.astype(jnp.bfloat16)
    lower = (table - upper.astype(np.float32)).astype(jnp.bfloat16)
    return upper, lower


def chirp_phase(row_pos, col_pos, row_total, col_total, factor):
    row_term = (row_pos - row_total / 2.0) ** 2 / row_total
    col_term = (col_pos - col_total / 2.0) ** 2 / col_total
    angle = math.pi * factor * (row_term[:, None] + col_term[None, :])
    return (jnp.cos(angle), jnp.sin(angle))


def column_tables(length, pix_count):
    table_re, table_im = dft_table(length)
    full = np.stack([np.stack([table_re, table_im], 1), np.stack([-table_im, table_re], 1)])
    full = full.reshape(2, length, 2, pix_count, length // pix_count).transpose(0, 1, 3, 2, 4)
    return np.stack(split(full.reshape(2 * length, 2 * length)))


def row_section(spectrum, share, col_pos, row_total, col_total):
    width = col_pos.shape[0]
    table_re, table_im = dft_table(row_total)
    upper, lower = split(np.concatenate([table_re, table_im], axis=0))
    tables = np.concatenate([upper, lower], axis=0)
    wide = jnp.dot(jnp.asarray(tables), spectrum, preferred_element_type=jnp.float32)
    wide = wide[: 2 * row_total] + wide[2 * row_total :]
    half = share * width
    out_re = wide[:row_total, :half] - wide[row_total:, half:]
    out_im = wide[:row_total, half:] + wide[row_total:, :half]
    row_pos = jnp.arange(row_total, dtype=jnp.float32)
    chirp_re, chirp_im = chirp_phase(row_pos, col_pos, row_total, col_total, 0.25)
    out_re = out_re.reshape(row_total, share, width).transpose(1, 0, 2)
    out_im = out_im.reshape(row_total, share, width).transpose(1, 0, 2)
    return jnp.stack([chirp_re * out_re - chirp_im * out_im, chirp_re * out_im + chirp_im * out_re])


def shards(wavefronts, trial_modes):
    rows_dev, cols = wavefronts.shape[2:]
    share = trial_modes.shape[1] // lax.axis_size("elec")
    pix_count = lax.axis_size("pix")
    row_total = rows_dev * pix_count
    tables = jnp.asarray(column_tables(cols, pix_count))
    column_block = middle(wavefronts, trial_modes, tables).reshape(row_total, -1)
    width = cols // pix_count
    col_pos = (lax.axis_index("pix") * width + jnp.arange(width, dtype=jnp.int32)).astype(
        jnp.float32
    )
    return row_section(column_block, share, col_pos, row_total, cols)


def solution(mesh):
    in_specs = (P("elec", None, "pix", None), P(None, None, "pix", None))
    out_specs = P(None, "elec", None, "pix")
    return jax.shard_map(shards, mesh=mesh, in_specs=in_specs, out_specs=out_specs, check_vma=False)
```

```python
import functools
import math

import jax
import jax.numpy as jnp
import numpy as np
from jax import lax
from jax.experimental import pallas as pl
from jax.experimental.pallas import tpu as pltpu
from jax.sharding import PartitionSpec as P

NS_STEPS = 8

HIGH = lax.Precision.HIGHEST
MESH = pl.DeviceIdType.MESH
EBLOCK = 128


def greet(*groups):
    barrier = pltpu.get_barrier_semaphore()
    for axis, peers in groups:
        for peer in peers:
            pl.semaphore_signal(barrier, inc=1, device_id={axis: peer}, device_id_type=MESH)
    return sum(len(peers) for _, peers in groups)


def remote(src, dst, send_sem, recv_sem, axis, peer):
    return pltpu.make_async_remote_copy(
        src_ref=src,
        dst_ref=dst,
        send_sem=send_sem,
        recv_sem=recv_sem,
        device_id={axis: peer},
        device_id_type=MESH,
    )


NT = (((1,), (1,)), ((), ()))
NN = (((1,), (0,)), ((), ()))


def dot(left, right, dims):
    return lax.dot_general(left, right, dims, preferred_element_type=jnp.float32)


def scatter_gather(n, peers, x_ref, held, out_ref, send_a, recv_a, send_b, recv_b, store):
    me = lax.axis_index("pix")
    started = []
    scatter = []
    for d in range(1, n):
        peer = peers[d - 1]
        copy = remote(x_ref.at[peer], held.at[d], send_a.at[d], recv_a.at[d], "pix", peer)
        copy.start()
        scatter.append(copy)
    total = x_ref[me].astype(jnp.float32)
    for d in range(1, n):
        scatter[d - 1].wait_recv()
        total = total + held[d].astype(jnp.float32)
    store(total)
    for d in range(1, n):
        copy = remote(
            out_ref.at[me], out_ref.at[me], send_b.at[d], recv_b.at[d], "pix", peers[d - 1]
        )
        copy.start()
        started.append(copy)
    for d in range(1, n):
        source = lax.rem(me + n - d, n)
        block = out_ref.at[source]
        remote(block, block, send_b.at[d], recv_b.at[d], "pix", source).wait_recv()
    return scatter + started


def core_kernel(
    np_, ne, pieces, sub, electrons, modes, raw,
    waves_hbm, trial_hbm, table_hbm,
    out_ref,
    stage_ref, waves_ref, trial_ref, low_ref, chirp_ref, table_ref, pick_ref,
    applied_ref, turn_ref, part_ref, lines_ref, launch_ref, spec_ref, send_ref, rows_a, both_ref, cut_ref, emb_ref,
    held_a, total_a, pay_ref, held_b, total_b,
    x_ref, pair, half, far, first_ref, gram_in,
    ps, es, gs, load_sem,
):
    share = modes // ne
    rows, cols = chirp_ref.shape[1:]
    pixels = rows * cols
    lines = sub // cols
    order = 2 * modes
    chunk = order // ne
    depth = order // np_
    width = pixels // pieces
    me_p = lax.axis_index("pix")
    peers = [lax.rem(me_p + d, np_) for d in range(1, np_)]
    me = lax.axis_index("elec")
    core = lax.rem(me, 2)
    chip = me // 2
    chips = ne // 2
    partner = chip * 2 + 1 - core
    others = [lax.rem(chip + d, chips) for d in range(1, chips)]
    seats = [other * 2 + core for other in others]
    sources = [lax.rem(chip + chips - d, chips) for d in range(1, chips)]
    greeted = greet(("pix", peers), ("elec", [partner] + seats))
    rows_a[...] = jnp.zeros_like(rows_a)

    def load(src, dst, slot):
        copy = pltpu.make_async_copy(src, dst, load_sem.at[slot])
        copy.start()
        return copy

    panels = cols // 128
    trial_copies = [
        load(trial_hbm.at[:, pl.ds(b * 128, 128)], trial_ref.at[b], 2 + b) for b in range(panels)
    ]
    if raw:
        band, batch = 8, EBLOCK
        blocks = electrons // batch

        def wave_copy(step):
            block, half_of = step // 2, lax.rem(step, 2)
            at = (pl.ds(pl.multiple_of(block * batch, batch), batch), half_of)
            return pltpu.make_async_copy(
                waves_hbm.at[at], stage_ref.at[at], load_sem.at[2 + panels + step]
            )

        for step in range(2 * blocks):
            wave_copy(step).start()
    else:
        wave_copy = load(waves_hbm, waves_ref, 2 + panels)
    table_copy = load(table_hbm, table_ref, 1)
    row_pos = (lax.broadcasted_iota(jnp.int32, (rows, 128), 0) + me_p * rows).astype(jnp.float32)
    col_pos = lax.broadcasted_iota(jnp.int32, (8, cols), 1).astype(jnp.float32)
    row_all = float(rows * np_)
    row_angle = (math.pi * 0.5) * (row_pos - row_all / 2.0) ** 2 / row_all
    col_angle = (math.pi * 0.5) * (col_pos - cols / 2.0) ** 2 / float(cols)
    row_cos, row_sin = jnp.cos(row_angle)[:, 0:1], jnp.sin(row_angle)[:, 0:1]
    col_cos, col_sin = jnp.cos(col_angle)[0:1], jnp.sin(col_angle)[0:1]
    chirp_ref[0] = row_cos * col_cos - row_sin * col_sin
    chirp_ref[1] = row_sin * col_cos + row_cos * col_sin
    for copy in trial_copies:
        copy.wait()

    def lower_modes(row, carry):
        fields = jnp.concatenate(
            [trial_ref[b, pl.ds(row, order, stride=rows), :] for b in range(panels)], axis=1
        ).astype(jnp.bfloat16)
        at = pl.ds(pl.multiple_of(row * cols, 128), cols)
        low_ref[:, at] = fields
        return carry

    lax.fori_loop(0, rows, lower_modes, 0)

    def wave(half_of, row, count):
        return jnp.concatenate([waves_ref[half_of * rows + row + i] for i in range(count)], axis=1)

    def correlate(fields, row):
        swapped = jnp.concatenate([-fields[modes:], fields[:modes]], axis=0)
        rows_a[:, 0:electrons] += dot(fields, wave(0, row, lines), NT) + dot(
            swapped, wave(1, row, lines), NT
        )

    if raw:
        tile = band * 32
        pick_row = lax.broadcasted_iota(jnp.int32, (tile, tile), 0)
        pick_col = lax.broadcasted_iota(jnp.int32, (tile, tile), 1)
        pick_ref[...] = jnp.where(
            pick_col == lax.rem(pick_row, 32) * band + pick_row // 32, 1.0, 0.0
        ).astype(jnp.bfloat16)

        def sort_block(step, carry):
            wave_copy(step).wait()
            block, half_of = step // 2, lax.rem(step, 2)
            base = pl.multiple_of(block * batch, batch)

            for band_of in range(rows // band):
                sorted_tiles = []
                for t in range(batch // 32):
                    mixed = stage_ref[pl.ds(base + t * 32, 32), half_of, band_of]
                    sorted_tiles.append(
                        dot(pick_ref[...], mixed.reshape(tile, cols), NN).astype(jnp.bfloat16)
                    )
                for r in range(band):
                    for t in range(batch // 32):
                        waves_ref[
                            half_of * rows + band_of * band + r, pl.ds(base + t * 32, 32), :
                        ] = sorted_tiles[t][r * 32 : (r + 1) * 32]
            return carry

        lax.fori_loop(0, 2 * blocks, sort_block, 0)
    else:
        wave_copy.wait()

    def opening(step, carry):
        at = pl.ds(pl.multiple_of(step * sub, 128), sub)
        correlate(low_ref[:, at], step * lines)
        return carry

    lax.fori_loop(0, rows // lines, opening, 0)
    table_copy.wait()
    for j in range(np_):
        part_ref[j] = rows_a[pl.ds(j * depth, depth), 0:electrons].astype(jnp.bfloat16)
    pl.semaphore_wait(pltpu.get_barrier_semaphore(), greeted)
    def store_first(total):
        total_a[me_p] = total.astype(jnp.bfloat16)

    def store_split(ref, lead, block):
        upper = block.astype(jnp.bfloat16)
        ref[lead] = upper
        ref[lead, :, electrons + order : electrons + 2 * order] = (
            block[:, electrons : electrons + order]
            - upper[:, electrons : electrons + order].astype(jnp.float32)
        ).astype(jnp.bfloat16)

    def store_second(total):
        gram = total[:, electrons : electrons + order] + total[:, electrons + order : electrons + 2 * order]
        rows_a[0:depth, 0:electrons] = total[:, 0:electrons]
        rows_a[0:depth, electrons : electrons + order] = gram
        store_split(total_b, me_p, rows_a[0:depth, :])

    started = scatter_gather(
        np_, peers, part_ref, held_a, total_a, ps.at[0], ps.at[1], ps.at[2], ps.at[3], store_first
    )
    for j in range(np_):
        rows_a[pl.ds(j * depth, depth), 0:electrons] = total_a[j].astype(jnp.float32)

    def part(ref, lead, piece):
        return ref.at[lead, :, pl.ds(piece * width, width)]

    def cut(piece):
        return pl.ds(piece * width, width)

    def round_trip(turn, gathered, finish, beside, scale=None):
        sa, ra, sb, rb, sc, rc, sd, rd, se, re = [es.at[10 * turn + i] for i in range(10)]
        first, second = {}, {}

        def compute(piece):
            def body(step, carry):
                start = pl.multiple_of(piece * width + step * sub, 128)
                row = (piece * (width // sub) + step) * lines
                both = both_ref[...]
                from_re = dot(both, wave(0, row, lines), NN)
                from_im = dot(both, wave(1, row, lines), NN)
                real = from_re[:modes] + from_im[modes:]
                imag = from_re[modes:] - from_im[:modes]
                if scale is not None:
                    real, imag = real * scale, imag * scale
                if chunk % 16 == 0:
                    whole = jnp.concatenate([real, imag], axis=0).astype(jnp.bfloat16)
                    for j in range(ne):
                        x_ref[turn, j, :, pl.ds(start, sub)] = whole[j * chunk : (j + 1) * chunk]
                else:
                    cut_ref[0:modes, :] = real
                    cut_ref[modes:order, :] = imag
                    for j in range(ne):
                        x_ref[turn, j, :, pl.ds(start, sub)] = cut_ref[
                            pl.ds(j * chunk, chunk), :
                        ].astype(jnp.bfloat16)
                return carry

            lax.fori_loop(0, width // sub, body, 0)
            for d, other in enumerate(others + [chip]):
                slot = d * pieces + piece
                copy = remote(
                    part(x_ref.at[turn], other * 2 + 1 - core, piece),
                    part(pair.at[turn], d, piece),
                    sa.at[slot], ra.at[slot], "elec", partner,
                )
                copy.start()
                started.append(copy)
                first[d, piece] = copy

        def cross(piece):
            for d in range(chips - 1):
                slot = d * pieces + piece
                first[d, piece].wait_recv()
                half[turn, d, :, cut(piece)] = (
                    x_ref[turn, seats[d], :, cut(piece)].astype(jnp.float32)
                    + pair[turn, d, :, cut(piece)].astype(jnp.float32)
                ).astype(jnp.bfloat16)
                copy = remote(
                    part(half.at[turn], d, piece), part(far.at[turn], d, piece),
                    sb.at[slot], rb.at[slot], "elec", seats[d],
                )
                copy.start()
                started.append(copy)
                second[d, piece] = copy

        def close(piece):
            first[chips - 1, piece].wait_recv()
            total = x_ref[turn, me, :, cut(piece)].astype(jnp.float32) + pair[
                turn, chips - 1, :, cut(piece)
            ].astype(jnp.float32)
            for d in range(chips - 1):
                second[d, piece].wait_recv()
                total = total + far[turn, d, :, cut(piece)].astype(jnp.float32)
            gathered[me, :, cut(piece)] = total.astype(jnp.bfloat16)
            block = part(gathered, me, piece)
            for d in range(chips - 1):
                slot = d * pieces + piece
                copy = remote(block, block, sc.at[slot], rc.at[slot], "elec", seats[d])
                copy.start()
                started.append(copy)
            copy = remote(block, block, sd.at[piece], rd.at[piece], "elec", partner)
            copy.start()
            started.append(copy)

        def relay(piece):
            for d in range(chips - 1):
                slot = d * pieces + piece
                source = sources[d] * 2 + core
                block = part(gathered, source, piece)
                remote(block, block, sc.at[slot], rc.at[slot], "elec", source).wait_recv()
                copy = remote(block, block, se.at[slot], re.at[slot], "elec", partner)
                copy.start()
                started.append(copy)

        def arrive(piece):
            block = part(gathered, partner, piece)
            remote(block, block, sd.at[piece], rd.at[piece], "elec", partner).wait_recv()
            for d in range(chips - 1):
                slot = d * pieces + piece
                block = part(gathered, sources[d] * 2 + 1 - core, piece)
                remote(block, block, se.at[slot], re.at[slot], "elec", partner).wait_recv()
            finish(piece)

        for tick in range(pieces + 5):
            for lag, stage in ((0, compute), (1, cross), (3, close), (4, relay), (5, arrive)):
                if 0 <= tick - lag < pieces:
                    stage(tick - lag)
            if tick == pieces:
                beside()

    def stacked(gathered, start):
        if chunk % 16 == 0:
            return jnp.concatenate([gathered[j, :, pl.ds(start, sub)] for j in range(ne)], axis=0)
        for j in range(ne):
            cut_ref[pl.ds(j * chunk, chunk), :] = gathered[j, :, pl.ds(start, sub)].astype(
                jnp.float32
            )
        return cut_ref[...].astype(jnp.bfloat16)

    both_ref[...] = rows_a[:, 0:electrons].astype(jnp.bfloat16)
    rows_a[...] = jnp.zeros_like(rows_a)

    def project_piece(piece):
        def body(step, carry):
            start = pl.multiple_of(piece * width + step * sub, 128)
            fields = stacked(first_ref, start)
            correlate(fields, (piece * (width // sub) + step) * lines)
            rows_a[:, electrons : electrons + order] += dot(fields, fields, NT)
            return carry

        lax.fori_loop(0, width // sub, body, 0)

    round_trip(0, first_ref, project_piece, lambda: None)
    for j in range(np_):
        store_split(pay_ref, j, rows_a[pl.ds(j * depth, depth), :])
    started += scatter_gather(
        np_, peers, pay_ref, held_b, total_b, ps.at[4], ps.at[5], ps.at[6], ps.at[7], store_second
    )
    for j in range(np_):
        rows_a[pl.ds(j * depth, depth), :] = total_b[j].astype(jnp.float32)

    row_id = lax.broadcasted_iota(jnp.int32, (order, order), 0)
    col_id = lax.broadcasted_iota(jnp.int32, (order, order), 1)
    raw = rows_a[:, electrons : electrons + order] + rows_a[:, electrons + order : electrons + 2 * order]
    trace = 2.0 * jnp.sum(
        jnp.sum(jnp.where(row_id == col_id, raw, 0.0), axis=1, keepdims=True), axis=0, keepdims=True
    )
    both_ref[...] = rows_a[:, 0:electrons].astype(jnp.bfloat16)
    scale = 1.0 / jnp.sqrt(trace)

    def first_turn():
        gram_re = raw[:modes, :modes] + raw[modes:, modes:]
        gram_im = raw[:modes, modes:] - raw[modes:, :modes]
        emb_ref[0:modes, 0:modes] = gram_re
        emb_ref[0:modes, modes:order] = -gram_im
        emb_ref[modes:order, 0:modes] = gram_im
        emb_ref[modes:order, modes:order] = gram_re
        identity = jnp.where(row_id == col_id, 1.0, 0.0).astype(jnp.float32)
        turn_ref[...] = newton_schulz(emb_ref[...] / trace, identity)

    emb2 = [jnp.zeros((order, order), jnp.float32)]

    def gram_piece(piece):
        def body(step, carry):
            fields = stacked(applied_ref, pl.multiple_of(piece * width + step * sub, 128))
            return carry + dot(fields, fields, NT)

        emb2[0] = lax.fori_loop(0, width // sub, body, emb2[0])

    round_trip(1, applied_ref, gram_piece, first_turn, scale)
    raw2 = emb2[0]
    gram_re = raw2[:modes, :modes] + raw2[modes:, modes:]
    gram_im = raw2[:modes, modes:] - raw2[modes:, :modes]
    low = modes // 2
    emb_ref[0:modes, 0:modes] = gram_re
    emb_ref[0:modes, modes:order] = gram_im
    gram_in[0, :, 0:order] = emb_ref[0:low, 0:order]
    gram_in[0, :, order : 2 * order] = emb_ref[low:modes, 0:order]
    last = []
    for d in range(1, np_):
        copy = remote(
            gram_in.at[0], gram_in.at[d], gs.at[0, d], gs.at[1, d], "pix", peers[d - 1]
        )
        copy.start()
        last.append(copy)
    total = gram_in[0]
    for d in range(1, np_):
        last[d - 1].wait_recv()
        total = total + gram_in[d]
    emb_ref[0:low, 0:order] = total[:, 0:order]
    emb_ref[low:modes, 0:order] = total[:, order : 2 * order]
    gram_re = emb_ref[0:modes, 0:modes]
    gram_im = emb_ref[0:modes, modes:order]
    emb_ref[0:modes, modes:order] = gram_im
    emb_ref[modes:order, 0:modes] = -gram_im
    emb_ref[modes:order, modes:order] = gram_re
    first_root = turn_ref[...]
    first_t = first_root.T
    raw = 0.5 * jnp.dot(
        jnp.dot(first_t, emb_ref[...], precision=HIGH), first_root, precision=HIGH
    )
    gram_re = raw[:modes, :modes] + raw[modes:, modes:]
    gram_im = raw[:modes, modes:] - raw[modes:, :modes]
    emb_ref[0:modes, 0:modes] = gram_re
    emb_ref[0:modes, modes:order] = -gram_im
    emb_ref[modes:order, 0:modes] = gram_im
    emb_ref[modes:order, modes:order] = gram_re
    embedded = emb_ref[...]
    diagonal = row_id == col_id
    trace = jnp.sum(
        jnp.sum(jnp.where(diagonal, embedded, 0.0), axis=1, keepdims=True), axis=0, keepdims=True
    )
    identity = jnp.where(diagonal, 1.0, 0.0).astype(jnp.float32)
    second_root = newton_schulz(embedded / trace, identity) / jnp.sqrt(trace)
    turn_ref[...] = jnp.dot(second_root.T, first_t, precision=HIGH)
    for part_of in range(2):
        emb_ref[pl.ds(part_of * share, share), :] = turn_ref[
            pl.ds(part_of * modes + me * share, share), :
        ]
    mine = emb_ref[0 : 2 * share, :]
    upper = mine.astype(jnp.bfloat16)
    lower = (mine - upper.astype(jnp.float32)).astype(jnp.bfloat16)
    group = next(count for count in (8, 5, 4, 2, 1) if rows % count == 0)

    def rotate(step, carry):
        start = pl.multiple_of(step * (group * cols), 128)
        if chunk % 16 == 0:
            fields = jnp.concatenate(
                [applied_ref[j, :, pl.ds(start, group * cols)] for j in range(ne)], axis=0
            )
        else:
            fields = jnp.concatenate(
                [
                    applied_ref[j, :, pl.ds(start, group * cols)].astype(jnp.float32)
                    for j in range(ne)
                ],
                axis=0,
            ).astype(jnp.bfloat16)
        turned = dot(upper, fields, NN) + dot(lower, fields, NN)
        for i in range(group):
            for b in range(cols // 128):
                lines_ref[b, pl.ds((step * group + i) * 2 * share, 2 * share), :] = turned[
                    :, i * cols + b * 128 : i * cols + (b + 1) * 128
                ]
        return carry

    lax.fori_loop(0, rows // group, rotate, 0)
    chirp_re, chirp_im = chirp_ref[0], chirp_ref[1]
    for m in range(share):
        real = jnp.concatenate(
            [lines_ref[b, pl.ds(m, rows, stride=2 * share), :] for b in range(cols // 128)], axis=1
        )
        imag = jnp.concatenate(
            [
                lines_ref[b, pl.ds(share + m, rows, stride=2 * share), :]
                for b in range(cols // 128)
            ],
            axis=1,
        )
        launch_ref[m * rows : (m + 1) * rows, 0:cols] = chirp_re * real - chirp_im * imag
        launch_ref[m * rows : (m + 1) * rows, cols : 2 * cols] = chirp_re * imag + chirp_im * real
    launch = launch_ref[...]
    upper = launch.astype(jnp.bfloat16)
    lower = (launch - upper.astype(jnp.float32)).astype(jnp.bfloat16)
    spec_ref[...] = (
        dot(upper, table_ref[0], NN) + dot(upper, table_ref[1], NN) + dot(lower, table_ref[0], NN)
    )
    thin = cols // np_
    for p in range(np_):
        for c in range(2):
            for m in range(share):
                at = (2 * p + c) * thin
                to = (c * share + m) * thin
                send_ref[p, :, to : to + thin] = spec_ref[
                    m * rows : (m + 1) * rows, at : at + thin
                ].astype(jnp.bfloat16)
    swaps = []
    for d in range(1, np_):
        copy = remote(
            send_ref.at[peers[d - 1]], out_ref.at[me_p], gs.at[2, d], gs.at[3, d], "pix",
            peers[d - 1],
        )
        copy.start()
        swaps.append(copy)
    out_ref[me_p] = send_ref[me_p]
    for d in range(1, np_):
        source = lax.rem(me_p + np_ - d, np_)
        block = out_ref.at[source]
        remote(block, block, gs.at[2, d], gs.at[3, d], "pix", source).wait_recv()
    for copy in started + last + swaps:
        copy.wait_send()


def middle(waves, trial, tables):
    np_ = lax.axis_size("pix")
    ne = lax.axis_size("elec")
    electrons, _, rows, cols = waves.shape
    mode_count = trial.shape[1]
    pixels = rows * cols
    order = 2 * mode_count
    chunk = order // ne
    depth = order // np_
    raw = rows % 8 == 0 and electrons % EBLOCK == 0
    if raw:
        waves = waves.reshape(electrons, 2, rows // 8, 8, cols)
        stage = waves.shape
    else:
        waves = waves.transpose(1, 2, 0, 3).reshape(2 * rows, electrons, cols)
        stage = (1, 1, 1, 8, 128)
    trial = trial.reshape(order * rows, cols)
    pieces = next(count for count in (4, 2, 1) if rows % count == 0)
    lines = next(size for size in (5, 4, 2, 1) if rows // pieces % size == 0)
    sub = lines * cols
    chips = ne // 2
    wide = electrons + 2 * order + -2 * order % 128
    share = mode_count // ne
    lanes = 2 * share * (cols // np_)
    vmem = pl.BlockSpec(memory_space=pltpu.VMEM)
    hbm = pl.BlockSpec(memory_space=pl.ANY)
    dma = pltpu.SemaphoreType.DMA
    f32, bf16 = jnp.float32, jnp.bfloat16
    return pl.pallas_call(
        functools.partial(core_kernel, np_, ne, pieces, sub, electrons, mode_count, raw),
        out_shape=jax.ShapeDtypeStruct((np_, rows, lanes), bf16),
        in_specs=[hbm] * 3,
        out_specs=vmem,
        scratch_shapes=[
            pltpu.VMEM(stage, bf16),
            pltpu.VMEM((2 * rows, electrons, cols), bf16),
            pltpu.VMEM((cols // 128, order * rows, 128), f32),
            pltpu.VMEM((order, pixels), bf16),
            pltpu.VMEM((2, rows, cols), f32),
            pltpu.VMEM(tables.shape, bf16),
            pltpu.VMEM((256, 256), bf16),
            pltpu.VMEM((ne, chunk, pixels), bf16),
            pltpu.VMEM((order, order), f32),
            pltpu.VMEM((np_, depth, electrons), bf16),
            pltpu.VMEM((cols // 128, rows * 2 * share, 128), f32),
            pltpu.VMEM((share * rows, 2 * cols), f32),
            pltpu.VMEM((share * rows, 2 * cols), f32),
            pltpu.VMEM((np_, rows, lanes), bf16),
            pltpu.VMEM((order, wide), f32),
            pltpu.VMEM((order, electrons), bf16),
            pltpu.VMEM((order, sub), f32),
            pltpu.VMEM((order, order), f32),
            pltpu.VMEM((np_, depth, electrons), bf16),
            pltpu.VMEM((np_, depth, electrons), bf16),
            pltpu.VMEM((np_, depth, wide), bf16),
            pltpu.VMEM((np_, depth, wide), bf16),
            pltpu.VMEM((np_, depth, wide), bf16),
            pltpu.VMEM((2, ne, chunk, pixels), bf16),
            pltpu.VMEM((2, chips, chunk, pixels), bf16),
            pltpu.VMEM((2, chips, chunk, pixels), bf16),
            pltpu.VMEM((2, chips, chunk, pixels), bf16),
            pltpu.VMEM((ne, chunk, pixels), bf16),
            pltpu.VMEM((np_, mode_count // 2, 2 * order), f32),
            dma((8, np_)),
            dma((20, chips * pieces)),
            dma((4, np_)),
            dma((2 + cols // 128 + max(1, 2 * electrons // EBLOCK),)),
        ],
        compiler_params=pltpu.CompilerParams(
            collective_id=1, has_side_effects=True, vmem_limit_bytes=60 * 1024 * 1024
        ),
        name="middle",
    )(waves, trial, tables)


def newton_schulz(scaled, identity):
    inverse_root = identity
    for step in range(NS_STEPS):
        product = scaled if step == 0 else jnp.dot(inverse_root, scaled, precision=HIGH)
        correction = 1.5 * identity - 0.5 * product
        if step == 0:
            inverse_root = correction
        else:
            inverse_root = jnp.dot(correction, inverse_root, precision=HIGH)
        if step + 1 < NS_STEPS:
            scaled = jnp.dot(scaled, correction, precision=HIGH)
    return inverse_root


def dft_table(length):
    index = np.arange(length, dtype=np.int64)
    angle = 2.0 * np.pi / length * (index[:, None] * index[None, :] % length)
    return np.cos(angle).astype(np.float32), -np.sin(angle).astype(np.float32)


def split(table):
    upper = table.astype(jnp.bfloat16)
    lower = (table - upper.astype(np.float32)).astype(jnp.bfloat16)
    return upper, lower


def chirp_phase(row_pos, col_pos, row_total, col_total, factor):
    row_term = (row_pos - row_total / 2.0) ** 2 / row_total
    col_term = (col_pos - col_total / 2.0) ** 2 / col_total
    angle = math.pi * factor * (row_term[:, None] + col_term[None, :])
    return (jnp.cos(angle), jnp.sin(angle))


def column_tables(length, pix_count):
    table_re, table_im = dft_table(length)
    full = np.stack([np.stack([table_re, table_im], 1), np.stack([-table_im, table_re], 1)])
    full = full.reshape(2, length, 2, pix_count, length // pix_count).transpose(0, 1, 3, 2, 4)
    return np.stack(split(full.reshape(2 * length, 2 * length)))


def row_section(spectrum, share, col_pos, row_total, col_total):
    width = col_pos.shape[0]
    table_re, table_im = dft_table(row_total)
    upper, lower = split(np.concatenate([table_re, table_im], axis=0))
    tables = np.concatenate([upper, lower], axis=0)
    wide = jnp.dot(jnp.asarray(tables), spectrum, preferred_element_type=jnp.float32)
    wide = wide[: 2 * row_total] + wide[2 * row_total :]
    half = share * width
    out_re = wide[:row_total, :half] - wide[row_total:, half:]
    out_im = wide[:row_total, half:] + wide[row_total:, :half]
    row_pos = jnp.arange(row_total, dtype=jnp.float32)
    chirp_re, chirp_im = chirp_phase(row_pos, col_pos, row_total, col_total, 0.25)
    out_re = out_re.reshape(row_total, share, width).transpose(1, 0, 2)
    out_im = out_im.reshape(row_total, share, width).transpose(1, 0, 2)
    return jnp.stack([chirp_re * out_re - chirp_im * out_im, chirp_re * out_im + chirp_im * out_re])


def shards(wavefronts, trial_modes):
    rows_dev, cols = wavefronts.shape[2:]
    share = trial_modes.shape[1] // lax.axis_size("elec")
    pix_count = lax.axis_size("pix")
    row_total = rows_dev * pix_count
    tables = jnp.asarray(column_tables(cols, pix_count))
    column_block = middle(wavefronts, trial_modes, tables).reshape(row_total, -1)
    width = cols // pix_count
    col_pos = (lax.axis_index("pix") * width + jnp.arange(width, dtype=jnp.int32)).astype(
        jnp.float32
    )
    return row_section(column_block, share, col_pos, row_total, cols)


def solution(mesh):
    in_specs = (P("elec", None, "pix", None), P(None, None, "pix", None))
    out_specs = P(None, "elec", None, "pix")
    return jax.shard_map(shards, mesh=mesh, in_specs=in_specs, out_specs=out_specs, check_vma=False)
```

```python
import functools
import math

import jax
import jax.numpy as jnp
import numpy as np
from jax import lax
from jax.experimental import pallas as pl
from jax.experimental.pallas import tpu as pltpu
from jax.sharding import PartitionSpec as P

NS_STEPS = 8

HIGH = lax.Precision.HIGHEST
MESH = pl.DeviceIdType.MESH
EBLOCK = 128


def greet(targets):
    barrier = pltpu.get_barrier_semaphore()
    for target in targets:
        pl.semaphore_signal(barrier, inc=1, device_id=target, device_id_type=MESH)
    return len(targets)


def remote(src, dst, send_sem, recv_sem, axis, peer=None):
    return pltpu.make_async_remote_copy(
        src_ref=src,
        dst_ref=dst,
        send_sem=send_sem,
        recv_sem=recv_sem,
        device_id=axis if peer is None else {axis: peer},
        device_id_type=MESH,
    )


NT = (((1,), (1,)), ((), ()))
NN = (((1,), (0,)), ((), ()))


def dot(left, right, dims):
    return lax.dot_general(left, right, dims, preferred_element_type=jnp.float32)


def scatter_gather(n, peers, x_ref, held, out_ref, send_a, recv_a, send_b, recv_b, store):
    me = lax.axis_index("pix")
    started = []
    scatter = []
    for d in range(1, n):
        peer = peers[d - 1]
        copy = remote(x_ref.at[peer], held.at[d], send_a.at[d], recv_a.at[d], "pix", peer)
        copy.start()
        scatter.append(copy)
    total = x_ref[me].astype(jnp.float32)
    for d in range(1, n):
        scatter[d - 1].wait_recv()
        total = total + held[d].astype(jnp.float32)
    store(total)
    for d in range(1, n):
        copy = remote(
            out_ref.at[me], out_ref.at[me], send_b.at[d], recv_b.at[d], "pix", peers[d - 1]
        )
        copy.start()
        started.append(copy)
    for d in range(1, n):
        source = lax.rem(me + n - d, n)
        block = out_ref.at[source]
        remote(block, block, send_b.at[d], recv_b.at[d], "pix", source).wait_recv()
    return scatter + started


def core_kernel(
    np_, ne, pieces, sub, electrons, modes, raw, bands,
    waves_hbm, trial_hbm, table_hbm,
    out_ref,
    stage_ref, waves_ref, trial_ref, low_ref, chirp_ref, table_ref, pick_ref,
    applied_ref, turn_ref, part_ref, lines_ref, launch_ref, spec_ref, send_ref, rows_a, both_ref, cut_ref, emb_ref,
    held_a, total_a, pay_ref, held_b, total_b,
    x_ref, pair, half, far, first_ref, gram_in,
    x2_ref, pair2, half2, far2, own_ref, gram_e, panel_ref, send2_ref,
    ps, es, gs, load_sem, ts, ge, fs,
):
    share = modes // ne
    rows, cols = chirp_ref.shape[1:]
    pixels = rows * cols
    lines = sub // cols
    order = 2 * modes
    chunk = order // ne
    depth = order // np_
    width = pixels // pieces
    me_p = lax.axis_index("pix")
    peers = [lax.rem(me_p + d, np_) for d in range(1, np_)]
    me = lax.axis_index("elec")
    core = lax.rem(me, 2)
    chip = me // 2
    chips = ne // 2
    partner = chip * 2 + 1 - core
    others = [lax.rem(chip + d, chips) for d in range(1, chips)]
    seats = [other * 2 + core for other in others]
    sources = [lax.rem(chip + chips - d, chips) for d in range(1, chips)]
    if bands:
        ring = [
            (de, dp, {"elec": lax.rem(me + de, ne), "pix": lax.rem(me_p + dp, np_)})
            for de in range(ne)
            for dp in range(np_)
            if de or dp
        ]
        greeted = greet([target for _, _, target in ring])
    else:
        greeted = greet(
            [{"pix": peer} for peer in peers] + [{"elec": peer} for peer in [partner] + seats]
        )
    rows_a[...] = jnp.zeros_like(rows_a)

    def load(src, dst, slot):
        copy = pltpu.make_async_copy(src, dst, load_sem.at[slot])
        copy.start()
        return copy

    panels = cols // 128
    trial_copies = [
        load(trial_hbm.at[:, pl.ds(b * 128, 128)], trial_ref.at[b], 2 + b) for b in range(panels)
    ]
    if raw:
        band, batch = 8, EBLOCK
        blocks = electrons // batch

        def wave_copy(step):
            block, half_of = step // 2, lax.rem(step, 2)
            at = (pl.ds(pl.multiple_of(block * batch, batch), batch), half_of)
            return pltpu.make_async_copy(
                waves_hbm.at[at], stage_ref.at[at], load_sem.at[2 + panels + step]
            )

        for step in range(2 * blocks):
            wave_copy(step).start()
    else:
        wave_copy = load(waves_hbm, waves_ref, 2 + panels)
    table_copy = load(table_hbm, table_ref, 1)
    row_pos = (lax.broadcasted_iota(jnp.int32, (rows, 128), 0) + me_p * rows).astype(jnp.float32)
    col_pos = lax.broadcasted_iota(jnp.int32, (8, cols), 1).astype(jnp.float32)
    row_all = float(rows * np_)
    row_angle = (math.pi * 0.5) * (row_pos - row_all / 2.0) ** 2 / row_all
    col_angle = (math.pi * 0.5) * (col_pos - cols / 2.0) ** 2 / float(cols)
    row_cos, row_sin = jnp.cos(row_angle)[:, 0:1], jnp.sin(row_angle)[:, 0:1]
    col_cos, col_sin = jnp.cos(col_angle)[0:1], jnp.sin(col_angle)[0:1]
    chirp_ref[0] = row_cos * col_cos - row_sin * col_sin
    chirp_ref[1] = row_sin * col_cos + row_cos * col_sin
    for copy in trial_copies:
        copy.wait()

    def lower_modes(row, carry):
        fields = jnp.concatenate(
            [trial_ref[b, pl.ds(row, order, stride=rows), :] for b in range(panels)], axis=1
        ).astype(jnp.bfloat16)
        at = pl.ds(pl.multiple_of(row * cols, 128), cols)
        low_ref[:, at] = fields
        return carry

    lax.fori_loop(0, rows, lower_modes, 0)

    def wave(half_of, row, count):
        return jnp.concatenate([waves_ref[half_of * rows + row + i] for i in range(count)], axis=1)

    def correlate(fields, row):
        swapped = jnp.concatenate([-fields[modes:], fields[:modes]], axis=0)
        rows_a[:, 0:electrons] += dot(fields, wave(0, row, lines), NT) + dot(
            swapped, wave(1, row, lines), NT
        )

    if raw:
        tile = band * 32
        pick_row = lax.broadcasted_iota(jnp.int32, (tile, tile), 0)
        pick_col = lax.broadcasted_iota(jnp.int32, (tile, tile), 1)
        pick_ref[...] = jnp.where(
            pick_col == lax.rem(pick_row, 32) * band + pick_row // 32, 1.0, 0.0
        ).astype(jnp.bfloat16)

        def sort_block(step, carry):
            wave_copy(step).wait()
            block, half_of = step // 2, lax.rem(step, 2)
            base = pl.multiple_of(block * batch, batch)

            for band_of in range(rows // band):
                sorted_tiles = []
                for t in range(batch // 32):
                    mixed = stage_ref[pl.ds(base + t * 32, 32), half_of, band_of]
                    sorted_tiles.append(
                        dot(pick_ref[...], mixed.reshape(tile, cols), NN).astype(jnp.bfloat16)
                    )
                for r in range(band):
                    for t in range(batch // 32):
                        waves_ref[
                            half_of * rows + band_of * band + r, pl.ds(base + t * 32, 32), :
                        ] = sorted_tiles[t][r * 32 : (r + 1) * 32]
            return carry

        lax.fori_loop(0, 2 * blocks, sort_block, 0)
    else:
        wave_copy.wait()

    def opening(step, carry):
        at = pl.ds(pl.multiple_of(step * sub, 128), sub)
        correlate(low_ref[:, at], step * lines)
        return carry

    lax.fori_loop(0, rows // lines, opening, 0)
    table_copy.wait()
    for j in range(np_):
        part_ref[j] = rows_a[pl.ds(j * depth, depth), 0:electrons].astype(jnp.bfloat16)
    pl.semaphore_wait(pltpu.get_barrier_semaphore(), greeted)
    def store_first(total):
        total_a[me_p] = total.astype(jnp.bfloat16)

    def store_split(ref, lead, block):
        upper = block.astype(jnp.bfloat16)
        ref[lead] = upper
        ref[lead, :, electrons + order : electrons + 2 * order] = (
            block[:, electrons : electrons + order]
            - upper[:, electrons : electrons + order].astype(jnp.float32)
        ).astype(jnp.bfloat16)

    def store_second(total):
        gram = total[:, electrons : electrons + order] + total[:, electrons + order : electrons + 2 * order]
        rows_a[0:depth, 0:electrons] = total[:, 0:electrons]
        rows_a[0:depth, electrons : electrons + order] = gram
        store_split(total_b, me_p, rows_a[0:depth, :])

    started = scatter_gather(
        np_, peers, part_ref, held_a, total_a, ps.at[0], ps.at[1], ps.at[2], ps.at[3], store_first
    )
    for j in range(np_):
        rows_a[pl.ds(j * depth, depth), 0:electrons] = total_a[j].astype(jnp.float32)

    def part(ref, lead, piece):
        return ref.at[lead, :, pl.ds(piece * width, width)]

    def cut(piece):
        return pl.ds(piece * width, width)

    def round_trip(turn, gathered, finish, beside, scale=None):
        sa, ra, sb, rb, sc, rc, sd, rd, se, re = [es.at[10 * turn + i] for i in range(10)]
        first, second = {}, {}

        def compute(piece):
            def body(step, carry):
                start = pl.multiple_of(piece * width + step * sub, 128)
                row = (piece * (width // sub) + step) * lines
                both = both_ref[...]
                from_re = dot(both, wave(0, row, lines), NN)
                from_im = dot(both, wave(1, row, lines), NN)
                real = from_re[:modes] + from_im[modes:]
                imag = from_re[modes:] - from_im[:modes]
                if scale is not None:
                    real, imag = real * scale, imag * scale
                if chunk % 16 == 0:
                    whole = jnp.concatenate([real, imag], axis=0).astype(jnp.bfloat16)
                    for j in range(ne):
                        x_ref[turn, j, :, pl.ds(start, sub)] = whole[j * chunk : (j + 1) * chunk]
                else:
                    cut_ref[0:modes, :] = real
                    cut_ref[modes:order, :] = imag
                    for j in range(ne):
                        x_ref[turn, j, :, pl.ds(start, sub)] = cut_ref[
                            pl.ds(j * chunk, chunk), :
                        ].astype(jnp.bfloat16)
                return carry

            lax.fori_loop(0, width // sub, body, 0)
            for d, other in enumerate(others + [chip]):
                slot = d * pieces + piece
                copy = remote(
                    part(x_ref.at[turn], other * 2 + 1 - core, piece),
                    part(pair.at[turn], d, piece),
                    sa.at[slot], ra.at[slot], "elec", partner,
                )
                copy.start()
                started.append(copy)
                first[d, piece] = copy

        def cross(piece):
            for d in range(chips - 1):
                slot = d * pieces + piece
                first[d, piece].wait_recv()
                half[turn, d, :, cut(piece)] = (
                    x_ref[turn, seats[d], :, cut(piece)].astype(jnp.float32)
                    + pair[turn, d, :, cut(piece)].astype(jnp.float32)
                ).astype(jnp.bfloat16)
                copy = remote(
                    part(half.at[turn], d, piece), part(far.at[turn], d, piece),
                    sb.at[slot], rb.at[slot], "elec", seats[d],
                )
                copy.start()
                started.append(copy)
                second[d, piece] = copy

        def close(piece):
            first[chips - 1, piece].wait_recv()
            total = x_ref[turn, me, :, cut(piece)].astype(jnp.float32) + pair[
                turn, chips - 1, :, cut(piece)
            ].astype(jnp.float32)
            for d in range(chips - 1):
                second[d, piece].wait_recv()
                total = total + far[turn, d, :, cut(piece)].astype(jnp.float32)
            gathered[me, :, cut(piece)] = total.astype(jnp.bfloat16)
            block = part(gathered, me, piece)
            for d in range(chips - 1):
                slot = d * pieces + piece
                copy = remote(block, block, sc.at[slot], rc.at[slot], "elec", seats[d])
                copy.start()
                started.append(copy)
            copy = remote(block, block, sd.at[piece], rd.at[piece], "elec", partner)
            copy.start()
            started.append(copy)

        def relay(piece):
            for d in range(chips - 1):
                slot = d * pieces + piece
                source = sources[d] * 2 + core
                block = part(gathered, source, piece)
                remote(block, block, sc.at[slot], rc.at[slot], "elec", source).wait_recv()
                copy = remote(block, block, se.at[slot], re.at[slot], "elec", partner)
                copy.start()
                started.append(copy)

        def arrive(piece):
            block = part(gathered, partner, piece)
            remote(block, block, sd.at[piece], rd.at[piece], "elec", partner).wait_recv()
            for d in range(chips - 1):
                slot = d * pieces + piece
                block = part(gathered, sources[d] * 2 + 1 - core, piece)
                remote(block, block, se.at[slot], re.at[slot], "elec", partner).wait_recv()
            finish(piece)

        for tick in range(pieces + 5):
            for lag, stage in ((0, compute), (1, cross), (3, close), (4, relay), (5, arrive)):
                if 0 <= tick - lag < pieces:
                    stage(tick - lag)
            if tick == pieces:
                beside()

    def stacked(gathered, start):
        if chunk % 16 == 0:
            return jnp.concatenate([gathered[j, :, pl.ds(start, sub)] for j in range(ne)], axis=0)
        for j in range(ne):
            cut_ref[pl.ds(j * chunk, chunk), :] = gathered[j, :, pl.ds(start, sub)].astype(
                jnp.float32
            )
        return cut_ref[...].astype(jnp.bfloat16)

    both_ref[...] = rows_a[:, 0:electrons].astype(jnp.bfloat16)
    rows_a[...] = jnp.zeros_like(rows_a)

    def project_piece(piece):
        def body(step, carry):
            start = pl.multiple_of(piece * width + step * sub, 128)
            fields = stacked(first_ref, start)
            correlate(fields, (piece * (width // sub) + step) * lines)
            rows_a[:, electrons : electrons + order] += dot(fields, fields, NT)
            return carry

        lax.fori_loop(0, width // sub, body, 0)

    round_trip(0, first_ref, project_piece, lambda: None)
    for j in range(np_):
        store_split(pay_ref, j, rows_a[pl.ds(j * depth, depth), :])
    started += scatter_gather(
        np_, peers, pay_ref, held_b, total_b, ps.at[4], ps.at[5], ps.at[6], ps.at[7], store_second
    )
    for j in range(np_):
        rows_a[pl.ds(j * depth, depth), :] = total_b[j].astype(jnp.float32)

    row_id = lax.broadcasted_iota(jnp.int32, (order, order), 0)
    col_id = lax.broadcasted_iota(jnp.int32, (order, order), 1)
    raw = rows_a[:, electrons : electrons + order] + rows_a[:, electrons + order : electrons + 2 * order]
    trace = 2.0 * jnp.sum(
        jnp.sum(jnp.where(row_id == col_id, raw, 0.0), axis=1, keepdims=True), axis=0, keepdims=True
    )
    both_ref[...] = rows_a[:, 0:electrons].astype(jnp.bfloat16)
    scale = 1.0 / jnp.sqrt(trace)

    def first_turn():
        gram_re = raw[:modes, :modes] + raw[modes:, modes:]
        gram_im = raw[:modes, modes:] - raw[modes:, :modes]
        emb_ref[0:modes, 0:modes] = gram_re
        emb_ref[0:modes, modes:order] = -gram_im
        emb_ref[modes:order, 0:modes] = gram_im
        emb_ref[modes:order, modes:order] = gram_re
        identity = jnp.where(row_id == col_id, 1.0, 0.0).astype(jnp.float32)
        turn_ref[...] = newton_schulz(emb_ref[...] / trace, identity)

    emb2 = [jnp.zeros((order, order), jnp.float32)]

    def gram_piece(piece):
        def body(step, carry):
            fields = stacked(applied_ref, pl.multiple_of(piece * width + step * sub, 128))
            return carry + dot(fields, fields, NT)

        emb2[0] = lax.fori_loop(0, width // sub, body, emb2[0])

    def split_trip():
        deep = rows // (bands * ne)
        span = deep * cols
        sa, ra, sb, rb = [ts.at[i] for i in range(4)]
        first, second = {}, {}

        def at(piece):
            return pl.ds(piece * span, span)

        def compute(piece):
            def body(step, carry):
                row = piece * ne * deep + step * 2 * deep
                both = both_ref[...]
                from_re = dot(both, wave(0, row, 2 * deep), NN)
                from_im = dot(both, wave(1, row, 2 * deep), NN)
                real = (from_re[:modes] + from_im[modes:]) * scale
                imag = (from_re[modes:] - from_im[:modes]) * scale
                whole = jnp.concatenate([real, imag], axis=0).astype(jnp.bfloat16)
                for k in range(2):
                    x2_ref[2 * step + k, :, at(piece)] = whole[:, k * span : (k + 1) * span]
                return carry

            lax.fori_loop(0, ne // 2, body, 0)
            for d, other in enumerate(others + [chip]):
                slot = d * bands + piece
                copy = remote(
                    x2_ref.at[other * 2 + 1 - core, :, at(piece)], pair2.at[d, :, at(piece)],
                    sa.at[slot], ra.at[slot], "elec", partner,
                )
                copy.start()
                started.append(copy)
                first[d, piece] = copy

        def cross(piece):
            for d in range(chips - 1):
                slot = d * bands + piece
                first[d, piece].wait_recv()
                half2[d, :, at(piece)] = (
                    x2_ref[seats[d], :, at(piece)].astype(jnp.float32)
                    + pair2[d, :, at(piece)].astype(jnp.float32)
                ).astype(jnp.bfloat16)
                copy = remote(
                    half2.at[d, :, at(piece)], far2.at[d, :, at(piece)],
                    sb.at[slot], rb.at[slot], "elec", seats[d],
                )
                copy.start()
                started.append(copy)
                second[d, piece] = copy

        def close(piece):
            first[chips - 1, piece].wait_recv()
            total = x2_ref[me, :, at(piece)].astype(jnp.float32) + pair2[
                chips - 1, :, at(piece)
            ].astype(jnp.float32)
            for d in range(chips - 1):
                second[d, piece].wait_recv()
                total = total + far2[d, :, at(piece)].astype(jnp.float32)
            own_ref[:, at(piece)] = total
            fields = total.astype(jnp.bfloat16)
            emb2[0] = emb2[0] + dot(fields, fields, NT)

        for tick in range(bands + 3):
            for lag, stage in ((0, compute), (1, cross), (3, close)):
                if 0 <= tick - lag < bands:
                    stage(tick - lag)
            if tick == bands:
                first_turn()

    if bands:
        split_trip()
    else:
        round_trip(1, applied_ref, gram_piece, first_turn, scale)
    raw2 = emb2[0]
    gram_re = raw2[:modes, :modes] + raw2[modes:, modes:]
    gram_im = raw2[:modes, modes:] - raw2[modes:, :modes]
    low = modes // 2
    emb_ref[0:modes, 0:modes] = gram_re
    emb_ref[0:modes, modes:order] = gram_im
    gram_in[0, :, 0:order] = emb_ref[0:low, 0:order]
    gram_in[0, :, order : 2 * order] = emb_ref[low:modes, 0:order]
    last = []
    if bands:
        gram_e[0] = gram_in[0]
        for d in range(1, ne):
            copy = remote(
                gram_e.at[0], gram_e.at[d], ge.at[0, d], ge.at[1, d], "elec", lax.rem(me + d, ne)
            )
            copy.start()
            last.append(copy)
        total = gram_e[0]
        for d in range(1, ne):
            last[d - 1].wait_recv()
            total = total + gram_e[d]
        gram_in[0] = total
    met = len(last)
    for d in range(1, np_):
        copy = remote(
            gram_in.at[0], gram_in.at[d], gs.at[0, d], gs.at[1, d], "pix", peers[d - 1]
        )
        copy.start()
        last.append(copy)
    total = gram_in[0]
    for d in range(1, np_):
        last[met + d - 1].wait_recv()
        total = total + gram_in[d]
    emb_ref[0:low, 0:order] = total[:, 0:order]
    emb_ref[low:modes, 0:order] = total[:, order : 2 * order]
    gram_re = emb_ref[0:modes, 0:modes]
    gram_im = emb_ref[0:modes, modes:order]
    emb_ref[0:modes, modes:order] = gram_im
    emb_ref[modes:order, 0:modes] = -gram_im
    emb_ref[modes:order, modes:order] = gram_re
    first_root = turn_ref[...]
    first_t = first_root.T
    raw = 0.5 * jnp.dot(
        jnp.dot(first_t, emb_ref[...], precision=HIGH), first_root, precision=HIGH
    )
    gram_re = raw[:modes, :modes] + raw[modes:, modes:]
    gram_im = raw[:modes, modes:] - raw[modes:, :modes]
    emb_ref[0:modes, 0:modes] = gram_re
    emb_ref[0:modes, modes:order] = -gram_im
    emb_ref[modes:order, 0:modes] = gram_im
    emb_ref[modes:order, modes:order] = gram_re
    embedded = emb_ref[...]
    diagonal = row_id == col_id
    trace = jnp.sum(
        jnp.sum(jnp.where(diagonal, embedded, 0.0), axis=1, keepdims=True), axis=0, keepdims=True
    )
    identity = jnp.where(diagonal, 1.0, 0.0).astype(jnp.float32)
    second_root = newton_schulz(embedded / trace, identity) / jnp.sqrt(trace)
    turn_ref[...] = jnp.dot(second_root.T, first_t, precision=HIGH)
    if bands:
        finish_split(
            np_, ne, bands, modes, rows, cols, ring, me, me_p, turn_ref[...], own_ref, chirp_ref,
            table_ref, launch_ref, panel_ref, send2_ref, out_ref, fs, started + last,
        )
        return
    for part_of in range(2):
        emb_ref[pl.ds(part_of * share, share), :] = turn_ref[
            pl.ds(part_of * modes + me * share, share), :
        ]
    mine = emb_ref[0 : 2 * share, :]
    upper = mine.astype(jnp.bfloat16)
    lower = (mine - upper.astype(jnp.float32)).astype(jnp.bfloat16)
    group = next(count for count in (8, 5, 4, 2, 1) if rows % count == 0)

    def rotate(step, carry):
        start = pl.multiple_of(step * (group * cols), 128)
        if chunk % 16 == 0:
            fields = jnp.concatenate(
                [applied_ref[j, :, pl.ds(start, group * cols)] for j in range(ne)], axis=0
            )
        else:
            fields = jnp.concatenate(
                [
                    applied_ref[j, :, pl.ds(start, group * cols)].astype(jnp.float32)
                    for j in range(ne)
                ],
                axis=0,
            ).astype(jnp.bfloat16)
        turned = dot(upper, fields, NN) + dot(lower, fields, NN)
        for i in range(group):
            for b in range(cols // 128):
                lines_ref[b, pl.ds((step * group + i) * 2 * share, 2 * share), :] = turned[
                    :, i * cols + b * 128 : i * cols + (b + 1) * 128
                ]
        return carry

    lax.fori_loop(0, rows // group, rotate, 0)
    chirp_re, chirp_im = chirp_ref[0], chirp_ref[1]
    for m in range(share):
        real = jnp.concatenate(
            [lines_ref[b, pl.ds(m, rows, stride=2 * share), :] for b in range(cols // 128)], axis=1
        )
        imag = jnp.concatenate(
            [
                lines_ref[b, pl.ds(share + m, rows, stride=2 * share), :]
                for b in range(cols // 128)
            ],
            axis=1,
        )
        launch_ref[m * rows : (m + 1) * rows, 0:cols] = chirp_re * real - chirp_im * imag
        launch_ref[m * rows : (m + 1) * rows, cols : 2 * cols] = chirp_re * imag + chirp_im * real
    launch = launch_ref[...]
    upper = launch.astype(jnp.bfloat16)
    lower = (launch - upper.astype(jnp.float32)).astype(jnp.bfloat16)
    spec_ref[...] = (
        dot(upper, table_ref[0], NN) + dot(upper, table_ref[1], NN) + dot(lower, table_ref[0], NN)
    )
    thin = cols // np_
    for p in range(np_):
        for c in range(2):
            for m in range(share):
                at = (2 * p + c) * thin
                to = (c * share + m) * thin
                send_ref[p, :, to : to + thin] = spec_ref[
                    m * rows : (m + 1) * rows, at : at + thin
                ].astype(jnp.bfloat16)
    swaps = []
    for d in range(1, np_):
        copy = remote(
            send_ref.at[peers[d - 1]], out_ref.at[me_p], gs.at[2, d], gs.at[3, d], "pix",
            peers[d - 1],
        )
        copy.start()
        swaps.append(copy)
    out_ref[me_p] = send_ref[me_p]
    for d in range(1, np_):
        source = lax.rem(me_p + np_ - d, np_)
        block = out_ref.at[source]
        remote(block, block, gs.at[2, d], gs.at[3, d], "pix", source).wait_recv()
    for copy in started + last + swaps:
        copy.wait_send()


def finish_split(
    np_, ne, bands, modes, rows, cols, ring, me, me_p, turn, own_ref, chirp_ref,
    table_ref, launch_ref, panel_ref, send2_ref, out_ref, fs, copies,
):
    deep = rows // (bands * ne)
    held = bands * deep
    share = modes // ne
    upper = turn.astype(jnp.bfloat16)
    lower = (turn - upper.astype(jnp.float32)).astype(jnp.bfloat16)
    for line in range(held):
        row = line // deep * ne * deep + me * deep + line % deep
        fields = own_ref[:, line * cols : (line + 1) * cols]
        big = fields.astype(jnp.bfloat16)
        small = (fields - big.astype(jnp.float32)).astype(jnp.bfloat16)
        turned = dot(upper, big, NN) + dot(lower, big, NN) + dot(upper, small, NN)
        real, imag = turned[:modes], turned[modes:]
        chirp_re = chirp_ref[0, pl.ds(row, 1), :]
        chirp_im = chirp_ref[1, pl.ds(row, 1), :]
        at = pl.ds(line * modes, modes)
        launch_ref[at, 0:cols] = chirp_re * real - chirp_im * imag
        launch_ref[at, cols : 2 * cols] = chirp_re * imag + chirp_im * real
    launch = launch_ref[...]
    big = launch.astype(jnp.bfloat16)
    small = (launch - big.astype(jnp.float32)).astype(jnp.bfloat16)
    spectrum = (
        dot(big, table_ref[0], NN) + dot(big, table_ref[1], NN) + dot(small, table_ref[0], NN)
    )
    for b in range(2 * cols // 128):
        panel_ref[b] = spectrum[:, b * 128 : (b + 1) * 128]
    for b in range(2 * cols // 128):
        for m in range(0, modes, 2):
            left = panel_ref[b, pl.ds(m, held, stride=modes), :]
            right = panel_ref[b, pl.ds(m + 1, held, stride=modes), :]
            to = m % share * 64
            for k in range(2):
                send2_ref[m // share, 2 * b + k, :, to : to + 128] = jnp.concatenate(
                    [left[:, k * 64 : k * 64 + 64], right[:, k * 64 : k * 64 + 64]], axis=1
                ).astype(jnp.bfloat16)
    swaps = []
    for de, dp, target in ring:
        copy = remote(
            send2_ref.at[target["elec"], target["pix"]], out_ref.at[me_p, me],
            fs.at[0, de, dp], fs.at[1, de, dp], target,
        )
        copy.start()
        swaps.append(copy)
    out_ref[me_p, me] = send2_ref[me, me_p]
    for de, dp, target in ring:
        block = out_ref.at[lax.rem(me_p + np_ - dp, np_), lax.rem(me + ne - de, ne)]
        remote(block, block, fs.at[0, de, dp], fs.at[1, de, dp], target).wait_recv()
    for copy in copies + swaps:
        copy.wait_send()


def band_count(rows, cols, np_, ne, modes):
    if ne % 2 or 2 * cols // np_ != 64 or modes // ne % 2:
        return 0
    return next((count for count in (5, 4, 2, 1) if rows % (count * ne) == 0), 0)


def middle(waves, trial, tables):
    np_ = lax.axis_size("pix")
    ne = lax.axis_size("elec")
    electrons, _, rows, cols = waves.shape
    mode_count = trial.shape[1]
    pixels = rows * cols
    order = 2 * mode_count
    chunk = order // ne
    depth = order // np_
    raw = rows % 8 == 0 and electrons % EBLOCK == 0
    if raw:
        waves = waves.reshape(electrons, 2, rows // 8, 8, cols)
        stage = waves.shape
    else:
        waves = waves.transpose(1, 2, 0, 3).reshape(2 * rows, electrons, cols)
        stage = (1, 1, 1, 8, 128)
    trial = trial.reshape(order * rows, cols)
    pieces = next(count for count in (4, 2, 1) if rows % count == 0)
    lines = next(size for size in (5, 4, 2, 1) if rows // pieces % size == 0)
    sub = lines * cols
    chips = ne // 2
    wide = electrons + 2 * order + -2 * order % 128
    share = mode_count // ne
    lanes = 2 * share * (cols // np_)
    bands = band_count(rows, cols, np_, ne, mode_count)
    turns = 1 if bands else 2
    held = rows // ne if bands else 8
    strip = held * cols
    old = 128 if bands else pixels
    spare = mode_count if bands else 8
    shape = (np_, ne, held, lanes) if bands else (np_, rows, lanes)
    vmem = pl.BlockSpec(memory_space=pltpu.VMEM)
    hbm = pl.BlockSpec(memory_space=pl.ANY)
    dma = pltpu.SemaphoreType.DMA
    f32, bf16 = jnp.float32, jnp.bfloat16
    return pl.pallas_call(
        functools.partial(core_kernel, np_, ne, pieces, sub, electrons, mode_count, raw, bands),
        out_shape=jax.ShapeDtypeStruct(shape, bf16),
        in_specs=[hbm] * 3,
        out_specs=vmem,
        scratch_shapes=[
            pltpu.VMEM(stage, bf16),
            pltpu.VMEM((2 * rows, electrons, cols), bf16),
            pltpu.VMEM((cols // 128, order * rows, 128), f32),
            pltpu.VMEM((order, pixels), bf16),
            pltpu.VMEM((2, rows, cols), f32),
            pltpu.VMEM(tables.shape, bf16),
            pltpu.VMEM((256, 256), bf16),
            pltpu.VMEM((ne, chunk, old), bf16),
            pltpu.VMEM((order, order), f32),
            pltpu.VMEM((np_, depth, electrons), bf16),
            pltpu.VMEM((cols // 128, rows * 2 * share, 128), f32),
            pltpu.VMEM((share * rows, 2 * cols), f32),
            pltpu.VMEM((share * rows, 2 * cols), f32),
            pltpu.VMEM((np_, rows, lanes), bf16),
            pltpu.VMEM((order, wide), f32),
            pltpu.VMEM((order, electrons), bf16),
            pltpu.VMEM((order, sub), f32),
            pltpu.VMEM((order, order), f32),
            pltpu.VMEM((np_, depth, electrons), bf16),
            pltpu.VMEM((np_, depth, electrons), bf16),
            pltpu.VMEM((np_, depth, wide), bf16),
            pltpu.VMEM((np_, depth, wide), bf16),
            pltpu.VMEM((np_, depth, wide), bf16),
            pltpu.VMEM((turns, ne, chunk, pixels), bf16),
            pltpu.VMEM((turns, chips, chunk, pixels), bf16),
            pltpu.VMEM((turns, chips, chunk, pixels), bf16),
            pltpu.VMEM((turns, chips, chunk, pixels), bf16),
            pltpu.VMEM((ne, chunk, pixels), bf16),
            pltpu.VMEM((np_, mode_count // 2, 2 * order), f32),
            pltpu.VMEM((ne, 2 * spare, strip), bf16),
            pltpu.VMEM((chips, 2 * spare, strip), bf16),
            pltpu.VMEM((chips, 2 * spare, strip), bf16),
            pltpu.VMEM((chips, 2 * spare, strip), bf16),
            pltpu.VMEM((2 * spare, strip), f32),
            pltpu.VMEM((ne, mode_count // 2, 2 * order), f32),
            pltpu.VMEM((2 * cols // 128, held * spare, 128), f32),
            pltpu.VMEM((ne, np_, held, lanes), bf16),
            dma((8, np_)),
            dma((20, chips * pieces)),
            dma((4, np_)),
            dma((2 + cols // 128 + max(1, 2 * electrons // EBLOCK),)),
            dma((4, chips * max(1, bands))),
            dma((2, ne)),
            dma((2, ne, np_)),
        ],
        compiler_params=pltpu.CompilerParams(
            collective_id=1, has_side_effects=True, vmem_limit_bytes=60 * 1024 * 1024
        ),
        name="middle",
    )(waves, trial, tables)


def newton_schulz(scaled, identity):
    inverse_root = identity
    for step in range(NS_STEPS):
        product = scaled if step == 0 else jnp.dot(inverse_root, scaled, precision=HIGH)
        correction = 1.5 * identity - 0.5 * product
        if step == 0:
            inverse_root = correction
        else:
            inverse_root = jnp.dot(correction, inverse_root, precision=HIGH)
        if step + 1 < NS_STEPS:
            scaled = jnp.dot(scaled, correction, precision=HIGH)
    return inverse_root


def dft_table(length):
    index = np.arange(length, dtype=np.int64)
    angle = 2.0 * np.pi / length * (index[:, None] * index[None, :] % length)
    return np.cos(angle).astype(np.float32), -np.sin(angle).astype(np.float32)


def split(table):
    upper = table.astype(jnp.bfloat16)
    lower = (table - upper.astype(np.float32)).astype(jnp.bfloat16)
    return upper, lower


def chirp_phase(row_pos, col_pos, row_total, col_total, factor):
    row_term = (row_pos - row_total / 2.0) ** 2 / row_total
    col_term = (col_pos - col_total / 2.0) ** 2 / col_total
    angle = math.pi * factor * (row_term[:, None] + col_term[None, :])
    return (jnp.cos(angle), jnp.sin(angle))


def column_tables(length, pix_count):
    table_re, table_im = dft_table(length)
    full = np.stack([np.stack([table_re, table_im], 1), np.stack([-table_im, table_re], 1)])
    full = full.reshape(2, length, 2, pix_count, length // pix_count).transpose(0, 1, 3, 2, 4)
    return np.stack(split(full.reshape(2 * length, 2 * length)))


def row_section(spectrum, share, col_pos, row_total, col_total):
    width = col_pos.shape[0]
    table_re, table_im = dft_table(row_total)
    upper, lower = split(np.concatenate([table_re, table_im], axis=0))
    tables = np.concatenate([upper, lower], axis=0)
    wide = jnp.dot(jnp.asarray(tables), spectrum, preferred_element_type=jnp.float32)
    wide = wide[: 2 * row_total] + wide[2 * row_total :]
    half = share * width
    out_re = wide[:row_total, :half] - wide[row_total:, half:]
    out_im = wide[:row_total, half:] + wide[row_total:, :half]
    row_pos = jnp.arange(row_total, dtype=jnp.float32)
    chirp_re, chirp_im = chirp_phase(row_pos, col_pos, row_total, col_total, 0.25)
    out_re = out_re.reshape(row_total, share, width).transpose(1, 0, 2)
    out_im = out_im.reshape(row_total, share, width).transpose(1, 0, 2)
    return jnp.stack([chirp_re * out_re - chirp_im * out_im, chirp_re * out_im + chirp_im * out_re])


def row_section_split(block, bands, share, col_pos, row_total, col_total):
    np_, ne, held, _ = block.shape
    deep = held // bands
    j, i, line = np.meshgrid(np.arange(np_), np.arange(ne), np.arange(held), indexing="ij")
    order = (j * held * ne + line // deep * ne * deep + i * deep + line % deep).reshape(-1)
    width = col_pos.shape[0]
    pad = -row_total % 128
    table = np.pad(np.stack(dft_table(row_total))[:, :, order], ((0, 0), (0, pad), (0, 0)))
    tables = jnp.asarray(np.concatenate(split(table.reshape(-1, row_total)), axis=0))
    wide = lax.dot_general(
        block.reshape(row_total, -1), tables, (((0,), (1,)), ((), ())),
        preferred_element_type=jnp.float32,
    )
    full = row_total + pad
    wide = wide[:, : 2 * full] + wide[:, 2 * full :]
    wide = wide.reshape(share, 2, width, 2 * full)
    first, second = wide[..., :row_total], wide[..., full : full + row_total]
    out_re = first[:, 0] - second[:, 1]
    out_im = second[:, 0] + first[:, 1]
    row_pos = jnp.arange(row_total, dtype=jnp.float32)
    chirp_re, chirp_im = chirp_phase(col_pos, row_pos, col_total, row_total, 0.25)
    out = jnp.stack([chirp_re * out_re - chirp_im * out_im, chirp_re * out_im + chirp_im * out_re])
    return out.transpose(0, 1, 3, 2)


def shards(wavefronts, trial_modes):
    rows_dev, cols = wavefronts.shape[2:]
    share = trial_modes.shape[1] // lax.axis_size("elec")
    pix_count = lax.axis_size("pix")
    row_total = rows_dev * pix_count
    tables = jnp.asarray(column_tables(cols, pix_count))
    column_block = middle(wavefronts, trial_modes, tables)
    width = cols // pix_count
    col_pos = (lax.axis_index("pix") * width + jnp.arange(width, dtype=jnp.int32)).astype(
        jnp.float32
    )
    bands = band_count(rows_dev, cols, pix_count, lax.axis_size("elec"), trial_modes.shape[1])
    if bands:
        return row_section_split(column_block, bands, share, col_pos, row_total, cols)
    return row_section(column_block.reshape(row_total, -1), share, col_pos, row_total, cols)


def solution(mesh):
    in_specs = (P("elec", None, "pix", None), P(None, None, "pix", None))
    out_specs = P(None, "elec", None, "pix")
    return jax.shard_map(shards, mesh=mesh, in_specs=in_specs, out_specs=out_specs, check_vma=False)
```
